32 devices in a mesh: dp: 8 (over z, core), tensor: 4 (over y, x).
Axes of the slice: x: 2, y: 2, z: 4, core: 2. Of those that a mesh axis runs over, the one named last changes fastest.
Arguments:
- tokens: bfloat16 [1024, 4096], P(('dp', 'tensor')), parts along dimension 0, may hold values from -6 to 6
- norm_gain: float32 [4096], replicated, may hold values from 0.1 to 1.9
- gate_w: bfloat16 [4096, 512], P(None, 'tensor'), may hold values from -0.09375 to 0.09375
- up_w: bfloat16 [4096, 512], P(None, 'tensor'), may hold values from -0.09375 to 0.09375
- down_w: bfloat16 [512, 4096], P('tensor'), may hold values from -0.25 to 0.25
- final_gain: float32 [4096], replicated, may hold values from 0.1 to 1.9
- vocab_w: bfloat16 [4608, 4096], P('tensor')
- targets: int32 [1024], P(('dp', 'tensor')), parts along dimension 0, may hold values from 0 to 4607
- lengths: int32 [8], P('dp'), parts along dimension 0, may hold values from 1 to 128
Outputs:
- losses: float32 [1024], P(('dp', 'tensor')), parts along dimension 0
The draws below stay inside these ranges and needn't reach their ends.
There are 8 independent parts, one for each index of `dp`. The reference program is written for one: setup_inputs(seed, part) draws one part's arguments, and reference() takes and returns one part's arrays. A program takes and returns all parts, laid end to end along the dimension named above; an argument that names none is the same for every part. Nothing has to cross between parts.
All inputs are finite; a program needn't handle non-finite values.
Results may differ from the reference program's by a relative error of at most 0.014.
Values may be sent and summed in bfloat16 or wider, within the bound.
A program may use at most 64 MiB of HBM per device.

```python
import math
import jax
import jax.numpy as jnp
from jax import lax

D = 4096
FF_DEV = 128
PACK_LEN = 128
TOKENS = 128
PACKS = 1
FF = 512
VOCAB = 4608
N_TENSOR = 4


def draw_vocab_w(key, part):
    key_base = jax.random.fold_in(jax.random.fold_in(key, 17), 0)
    weights = jax.random.normal(key_base, (VOCAB, D), jnp.float32) * (3.0 / math.sqrt(D))
    return weights.astype(jnp.bfloat16)


def place_ends(entries, key, least, high):
    longest = entries.shape.index(max(entries.shape))
    spots = []
    for shift in (0, 1):
        where = [jax.random.randint(jax.random.fold_in(key, axis), (), 0, length) for axis, length in enumerate(entries.shape)]
        where[longest] = (where[longest] + shift) % entries.shape[longest]
        spots.append(tuple(where))
    return entries.at[spots[0]].set(least).at[spots[1]].set(high)


def levels(rng, dims, pieces, least, largest):
    gain, own = 1.0, jax.random.fold_in(rng, 6)
    for axis_at, parts in pieces:
        heights = jnp.exp(jax.random.uniform(jax.random.fold_in(own, axis_at), (parts,), jnp.float32, least / len(pieces), largest / len(pieces)))
        gain = gain * jnp.repeat(heights, dims[axis_at] // parts).reshape([-1 if axis == axis_at else 1 for axis in range(len(dims))])
    return gain


def bell_draw(stream_key, dims, spread, limit, cuts=(), kind=jnp.bfloat16):
    entries = jax.random.normal(stream_key, dims, jnp.float32) * spread
    if len(cuts) > 0:
        entries = levels(stream_key, dims, cuts, -0.22, 0.18) * entries
    return jnp.clip(entries, min=-limit, max=limit).astype(kind)


def setup_inputs(seed: int = 0, part: int = 0) -> dict:
    arg_keys = jax.random.split(jax.random.key(seed), 10)
    part_splits = jax.random.split(jax.random.fold_in(arg_keys[9], part), 10)
    tokens = bell_draw(part_splits[0], (TOKENS, D), 1.0, 6.0, ((0, 4),))
    norm_gain = jnp.clip(1.0 + 0.18 * jax.random.normal(arg_keys[1], (D,), jnp.float32), 0.1, 1.9)
    gate_w = bell_draw(arg_keys[2], (D, FF), D ** -0.5, 0.09375, ((1, 4),))
    up_w = bell_draw(arg_keys[3], (D, FF), D ** -0.5, 0.09375, ((1, 4),))
    down_w = bell_draw(arg_keys[4], (FF, D), FF ** -0.5, 0.25, ((0, 4),))
    final_gain = jnp.clip(1.0 + 0.18 * jax.random.normal(arg_keys[5], (D,), jnp.float32), 0.1, 1.9)
    vocab_w = draw_vocab_w(jax.random.fold_in(arg_keys[9], 71), part)
    targets = place_ends(jax.random.randint(part_splits[7], (TOKENS,), 0, VOCAB), jax.random.fold_in(part_splits[7], 1), 0, VOCAB - 1).astype(jnp.int32)
    lengths = jax.random.randint(part_splits[8], (PACKS,), 1, PACK_LEN + 1).astype(jnp.int32)
    return {"tokens": tokens, "norm_gain": norm_gain, "gate_w": gate_w, "up_w": up_w, "down_w": down_w, "final_gain": final_gain, "vocab_w": vocab_w, "targets": targets, "lengths": lengths}


def scaled_norm(values, scale_gain):
    widened = values.astype(jnp.float32)
    return widened * lax.rsqrt(lax.optimization_barrier(jnp.mean(widened * widened, axis=1, keepdims=True)) + 1e-06) * scale_gain

def reference(tokens, norm_gain, gate_w, up_w, down_w, final_gain, vocab_w, targets, lengths):
    normed = scaled_norm(tokens, norm_gain).astype(jnp.bfloat16)
    gate_vals = jnp.dot(normed, gate_w, preferred_element_type=jnp.float32)
    up_vals = jnp.dot(normed, up_w, preferred_element_type=jnp.float32)
    hidden = (jax.nn.silu(gate_vals) * up_vals).astype(jnp.bfloat16)

    def add_block(block_index, running):
        begin = jnp.asarray(block_index * FF_DEV).astype(jnp.int32)
        hidden_part = lax.dynamic_slice_in_dim(hidden, begin, FF_DEV, 1)
        weight_part = lax.dynamic_slice_in_dim(down_w, begin, FF_DEV, 0)
        term = jnp.dot(hidden_part, weight_part, preferred_element_type=jnp.float32).astype(jnp.bfloat16)
        term = lax.optimization_barrier(term)
        return running + term.astype(jnp.float32)
    branch_sum = lax.fori_loop(0, N_TENSOR, add_block, jnp.zeros((TOKENS, D), jnp.float32))
    summed = (tokens.astype(jnp.float32) + branch_sum).astype(jnp.bfloat16)
    final_rows = scaled_norm(summed, final_gain).astype(jnp.bfloat16)
    logits = jnp.dot(final_rows, vocab_w.T, preferred_element_type=jnp.float32)
    row_max = lax.optimization_barrier(jnp.max(logits, axis=1))
    log_total = row_max + jnp.log(lax.optimization_barrier(jnp.sum(jnp.exp(logits - row_max[:, None]), axis=1)))
    target_logit = jnp.take_along_axis(logits, targets[:, None].astype(jnp.int32), axis=1)[:, 0]
    positions = jnp.arange(TOKENS, dtype=jnp.int32)
    pack_ids = (positions // PACK_LEN).astype(jnp.int32)
    limits = lengths[pack_ids]
    valid = positions % PACK_LEN < limits
    return jnp.where(valid, log_total - target_logit, jnp.float32(0.0))
```

```python
import functools

import jax
import jax.numpy as jnp
from jax import lax
from jax.experimental import pallas as pl
from jax.experimental.pallas import tpu as pltpu
from jax.sharding import PartitionSpec as P

PACK_LEN = 128
EPS = 1e-06
SHRINK = 2.0**-27
GROW = 2.0**27
F32, BF16 = jnp.float32, jnp.bfloat16
NT = (((1,), (1,)), ((), ()))


def dot(a, b):
    return jnp.dot(a, b, preferred_element_type=F32)


def dot_nt(a, b):
    return lax.dot_general(a, b, NT, preferred_element_type=F32)


def diagonal(rows):
    shape = (rows, rows)
    return lax.broadcasted_iota(jnp.int32, shape, 0) == lax.broadcasted_iota(jnp.int32, shape, 1)


def to_column(row):
    n = row.shape[1]
    return jnp.sum(jnp.where(diagonal(n), row, jnp.zeros_like(row)), axis=1, keepdims=True)


def to_row(column):
    n = column.shape[0]
    return jnp.sum(jnp.where(diagonal(n), column, jnp.zeros_like(column)), axis=0, keepdims=True)


def kernel(
    n_t, n_s, tile,
    tok_in, ng, gate_in, up_in, down_in, fg, voc_in, tgt, lens,
    out,
    tok, sl, gu, dw, voc, xn, xg, sg, sgo, x2, cross, logit, w2, gram, glow, tg, tgc, hid, qs, sts, sta,
    local_sem, voc_sem, t_send, t_recv, r_send, r_recv, s_send, s_recv,
):
    me = lax.axis_index("tensor")
    dp = lax.axis_index("dp")
    slot = lax.rem(dp, n_s)
    group = dp - slot
    _, tl, d = tok.shape
    rows = sl.shape[1]
    f = dw.shape[0]
    v = voc.shape[0]
    total = n_t * tl
    n_v = v // tile

    def local(i, src, dst):
        copy = pltpu.make_async_copy(src, dst, local_sem.at[i])
        copy.start()
        return copy

    own_rows = pl.ds(pl.multiple_of(slot * rows, rows), rows)
    own_tok = local(0, tok_in, tok.at[me])

    barrier = pltpu.get_barrier_semaphore()
    for k in range(1, n_t):
        pl.semaphore_signal(barrier, inc=1, device_id={"tensor": lax.rem(me + k, n_t)})
    n_z = n_s // 2
    z, core = slot // 2, lax.rem(slot, 2)
    sibling = 2 * z + 1 - core
    pl.semaphore_signal(barrier, inc=1, device_id={"dp": group + sibling})

    @pl.when(z > 0)
    def _():
        pl.semaphore_signal(barrier, inc=1, device_id={"dp": group + slot - 2})

    @pl.when(z < n_z - 1)
    def _():
        pl.semaphore_signal(barrier, inc=1, device_id={"dp": group + slot + 2})


    down_copy = local(1, down_in, dw)

    def voc_copy(c):
        part = pl.ds(pl.multiple_of(c * tile, tile), tile)
        return pltpu.make_async_copy(voc_in.at[part], voc.at[part], voc_sem.at[c])

    for c in range(n_v):
        voc_copy(c).start()
    gate_copy = local(2, gate_in, gu.at[:, pl.ds(0, f)])
    up_copy = local(3, up_in, gu.at[:, pl.ds(f, f)])
    tg[me] = jnp.broadcast_to(tgt[...], tg.shape[1:])
    beside = (z + n_z - 1) // n_z + (2 * n_z - 2 - z) // n_z
    pl.semaphore_wait(barrier, n_t + beside)

    def t_copy(kind, k, src, dst):
        return pltpu.make_async_remote_copy(
            src_ref=src, dst_ref=dst, send_sem=t_send.at[kind, k], recv_sem=t_recv.at[kind, k],
            device_id={"tensor": lax.rem(me + k, n_t)},
        )

    def piece(kind, j):
        part = pl.ds(pl.multiple_of(j * rows, rows), rows)
        if kind == 0:
            return gram.at[pl.ds(1, n_t - 1), part, :]
        return w2.at[pl.ds(1, n_t - 1), part, pl.ds((kind - 1) * tile, tile)]

    def s_copy(kind, j, way, to):
        return pltpu.make_async_remote_copy(
            src_ref=piece(kind, j), dst_ref=piece(kind, j),
            send_sem=s_send.at[kind, j, way], recv_sem=s_recv.at[kind, j],
            device_id={"dp": group + to},
        )

    def s_hop(kind, j, step, act):
        if step <= 0:
            @pl.when(z > 0)
            def _():
                act(s_copy(kind, j, 0, slot - 2))
        if step >= 0:
            @pl.when(z < n_z - 1)
            def _():
                act(s_copy(kind, j, 1, slot + 2))
        act(s_copy(kind, j, 2, sibling))

    def start(copy):
        copy.start()

    def wait_send(copy):
        copy.wait_send()

    def s_relay(kind, step):
        @pl.when(z - step >= 0)
        def _():
            j = slot - 2 * step
            s_copy(kind, j, 1, sibling).wait_recv()
            s_hop(kind, j, 1, start)

        @pl.when(z + step <= n_z - 1)
        def _():
            j = slot + 2 * step
            s_copy(kind, j, 0, sibling).wait_recv()
            s_hop(kind, j, -1, start)

    def s_arrived(kind):
        for other in range(n_z):
            s_copy(kind, 2 * other + 1 - core, 2, sibling).wait_recv()

    def s_sent(kind):
        s_hop(kind, slot, 0, wait_send)
        for step in range(1, n_z):
            @pl.when(z - step >= 0)
            def _():
                s_hop(kind, slot - 2 * step, 1, wait_send)

            @pl.when(z + step <= n_z - 1)
            def _():
                s_hop(kind, slot + 2 * step, -1, wait_send)

    def block(k):
        return lax.rem(me + k, n_t)

    def t_start(kind, src, dst):
        copies = [t_copy(kind, k, src(k), dst(k)) for k in range(1, n_t)]
        for copy in copies:
            copy.start()
        return copies

    relayed = n_t == 4
    if relayed:
        y, x = me // 2, lax.rem(me, 2)
        x_near, y_near, far = 2 * y + 1 - x, 2 * (1 - y) + x, 2 * (1 - y) + 1 - x

    def half(ref, h):
        return ref.at[:, pl.ds(h * (d // 2), d // 2)]

    def r_copies(kind, src, buf, place):
        plan = (
            (half(src, 0), me, 0, x_near), (half(src, 1), me, 1, x_near),
            (half(src, 1), me, 1, y_near), (half(src, 0), me, 0, y_near),
            (half(buf.at[place(y_near, me)], 1), y_near, 1, x_near),
            (half(buf.at[place(x_near, me)], 0), x_near, 0, y_near),
        )
        return [
            pltpu.make_async_remote_copy(
                src_ref=part, dst_ref=half(buf.at[place(owner, to)], h), send_sem=r_send.at[kind, i],
                recv_sem=r_recv.at[kind, i], device_id={"tensor": to},
            )
            for i, (part, owner, h, to) in enumerate(plan)
        ]

    def r_start(copies):
        for i in (0, 2, 1, 3):
            copies[i].start()

    def r_pass(copies):
        copies[0].wait_recv()
        copies[5].start()
        copies[2].wait_recv()
        copies[4].start()

    down_rows = down_in.at[own_rows]
    if relayed:
        sl_copies = r_copies(0, down_rows, sl, lambda owner, to: lax.rem(owner - to + n_t, n_t))
        tok_copies = r_copies(1, tok_in, tok, lambda owner, to: owner)
        r_start(sl_copies)
    else:
        sl_copies = t_start(0, lambda k: down_rows, lambda k: sl.at[n_t - k])
        tok_copies = t_start(1, lambda k: tok_in, lambda k: tok.at[me])

    def token_block(index):
        part = pl.ds(pl.multiple_of(index * tl, tl), tl)
        x = tok[index].astype(F32)
        square = jnp.sum(x * x, axis=1, keepdims=True)
        x2[part, :] = jnp.broadcast_to(square, (tl, x2.shape[1]))
        xn[part, :] = (x * lax.rsqrt(square * (1.0 / d) + EPS) * ng[...]).astype(BF16)
        xg[part, :] = (x * (fg[...] * SHRINK)).astype(BF16)

    tg_copies = t_start(2, lambda k: tg.at[me], lambda k: tg.at[me])
    own_tok.wait()
    token_block(me)
    down_copy.wait()
    sgo[...] = (dw[...].astype(F32) * (fg[...] * SHRINK)).astype(BF16)

    def own_w2(c):
        voc_copy(c).wait()
        part = pl.ds(c * tile, tile)
        w2[0, :, part] = dot_nt(sgo[...], voc[part, :]).astype(BF16)

    own_w2(0)
    if relayed:
        r_pass(sl_copies)
        r_start(tok_copies)
    for c in range(1, n_v):
        own_w2(c)
    own_gram = dot_nt(dw[...], dw[...])
    own_high = own_gram.astype(BF16)
    gram[0] = own_high
    glow[...] = (own_gram - own_high.astype(F32)).astype(BF16)

    for i, copy in enumerate(sl_copies):
        if not (relayed and i in (0, 2)):
            copy.wait_recv()
    raw = sl[pl.ds(1, n_t - 1)].reshape((n_t - 1) * rows, d)
    gram[pl.ds(1, n_t - 1), own_rows, :] = dot_nt(raw, dw[...]).astype(BF16).reshape(n_t - 1, rows, f)
    s_hop(0, slot, 0, start)
    sg[...] = (raw.astype(F32) * (fg[...] * SHRINK)).astype(BF16)
    for c in range(n_v):
        part = pl.ds(c * tile, tile)
        w2[pl.ds(1, n_t - 1), own_rows, part] = dot_nt(sg[...], voc[part, :]).astype(BF16).reshape(n_t - 1, rows, tile)
        s_hop(1 + c, slot, 0, start)
        if relayed and c == n_v // 2:
            r_pass(tok_copies)

    kinds = range(n_v + 1)
    if relayed:
        for needed, index in ((1, x_near), (3, y_near)):
            tok_copies[needed].wait_recv()
            token_block(index)
        for kind in kinds[:-1]:
            s_relay(kind, 1)
        for i in (4, 5):
            tok_copies[i].wait_recv()
        token_block(far)
    else:
        for k, copy in enumerate(tok_copies, 1):
            copy.wait_recv()
            token_block(lax.rem(me + n_t - k, n_t))
        for kind in kinds[:-1]:
            s_relay(kind, 1)

    gate_copy.wait()
    up_copy.wait()
    both = dot(xn[...], gu[...])
    gate, up = both[:, :f], both[:, f:]
    own_hidden = (gate / (1.0 + jnp.exp(-gate)) * up).astype(BF16)
    hid[me] = own_hidden
    h_copies = t_start(3, lambda k: hid.at[me], lambda k: hid.at[me])
    s_relay(kinds[-1], 1)
    s_relay(0, 2)
    cross[...] = dot_nt(tok[...].reshape(total, d), dw[...])

    def token_logits(c):
        part = pl.ds(c * tile, tile)
        logit[:, part] = dot_nt(xg[...], voc[part, :])

    for c in range(n_v - 1):
        s_relay(1 + c, 2)
        token_logits(c)
    for step in range(3, n_z):
        s_relay(0, step)
    for copy in h_copies:
        copy.wait_recv()
    s_arrived(0)
    hidden = jnp.concatenate([hid[block(k)] for k in range(n_t)], axis=1)
    pulled = dot(hidden, gram[...].reshape(n_t * f, f)) + dot(hid[me], glow[...])
    share = jnp.sum(hid[me].astype(F32) * (2.0 * cross[...] + pulled), axis=1, keepdims=True)
    qs[me] = jnp.broadcast_to(to_row(share), qs.shape[1:])
    q_copies = t_start(4, lambda k: qs.at[me], lambda k: qs.at[me])

    s_relay(n_v, 2)
    token_logits(n_v - 1)
    for step in range(3, n_z):
        for kind in kinds[1:]:
            s_relay(kind, step)
    for c in range(n_v):
        s_arrived(1 + c)
        part = pl.ds(c * tile, tile)
        logit[:, part] += dot(hidden, w2[:, :, part].reshape(n_t * f, tile))

    for copy in tg_copies:
        copy.wait_recv()
    for t in range(n_t):
        tgc[pl.ds(t * tl, tl), :] = jnp.broadcast_to(to_column(tg[t][0:1, :]), (tl, tgc.shape[1]))
    for copy in q_copies:
        copy.wait_recv()
    pulls = qs[0, 0:1, :]
    for t in range(1, n_t):
        pulls = pulls + qs[t, 0:1, :]
    square = jnp.maximum(x2[:, 0:1] + to_column(pulls), 0.0)
    x2[...] = jnp.broadcast_to(lax.rsqrt(square * (1.0 / d) + EPS) * GROW, x2.shape)

    @pl.loop(0, n_t, unroll=min(n_t, 4))
    def _(t):
        part = pl.ds(pl.multiple_of(t * tl, tl), tl)
        scaled = logit[part, :] * x2[part, 0:1]
        top = jnp.max(scaled, axis=1, keepdims=True)
        mass = jnp.sum(jnp.exp(scaled - top), axis=1, keepdims=True)
        columns = lax.broadcasted_iota(jnp.int32, (tl, v), 1) + me * v
        hit = jnp.sum(jnp.where(columns == tgc[part, 0:1], scaled, 0.0), axis=1, keepdims=True)
        sts[t, 0:1, :] = to_row(top)
        sts[t, 1:2, :] = to_row(mass)
        sts[t, 2:3, :] = to_row(hit)

    end = t_start(5, lambda k: sts.at[block(k)], lambda k: sta.at[me])
    sta[me] = sts[me]
    positions = me * tl + lax.broadcasted_iota(jnp.int32, (1, tl), 1)
    packs = positions // PACK_LEN
    limits = jnp.zeros((1, tl), jnp.int32)
    for i in range(lens.shape[0]):
        limits = jnp.where(packs == i, lens[i], limits)
    for copy in end:
        copy.wait_recv()
    stats = [sta[t] for t in range(n_t)]
    top = stats[0][0:1, :]
    for s in stats[1:]:
        top = jnp.maximum(top, s[0:1, :])
    mass = sum(s[1:2, :] * jnp.exp(s[0:1, :] - top) for s in stats)
    hit = sum(s[2:3, :] for s in stats)
    out[...] = jnp.where(positions - packs * PACK_LEN < limits, top + jnp.log(mass) - hit, 0.0)

    for copies in (sl_copies, tok_copies, tg_copies, h_copies, q_copies, end):
        for copy in copies:
            copy.wait_send()
    for kind in kinds:
        s_sent(kind)


def body(n_t, n_dp, tokens, norm_gain, gate_w, up_w, down_w, final_gain, vocab_w, targets, lengths):
    tl, d = tokens.shape
    f = down_w.shape[0]
    v = vocab_w.shape[0]
    n_s = min(n_dp, f // 16)
    rows = f // n_s
    total = n_t * tl
    tile = next(size for size in (384, 256, 128) if v % size == 0)
    vmem = pl.BlockSpec(memory_space=pltpu.VMEM)
    hbm = pl.BlockSpec(memory_space=pl.ANY)
    losses = pl.pallas_call(
        functools.partial(kernel, n_t, n_s, tile),
        out_shape=jax.ShapeDtypeStruct((1, tl), F32),
        in_specs=[hbm, vmem, hbm, hbm, hbm, vmem, hbm, vmem, pl.BlockSpec(memory_space=pltpu.SMEM)],
        out_specs=vmem,
        scratch_shapes=[
            pltpu.VMEM((n_t, tl, d), BF16),
            pltpu.VMEM((n_t, rows, d), BF16),
            pltpu.VMEM((d, 2 * f), BF16),
            pltpu.VMEM((f, d), BF16),
            pltpu.VMEM((v, d), BF16),
            pltpu.VMEM((total, d), BF16),
            pltpu.VMEM((total, d), BF16),
            pltpu.VMEM(((n_t - 1) * rows, d), BF16),
            pltpu.VMEM((f, d), BF16),
            pltpu.VMEM((total, 128), F32),
            pltpu.VMEM((total, f), F32),
            pltpu.VMEM((total, v), F32),
            pltpu.VMEM((n_t, f, v), BF16),
            pltpu.VMEM((n_t, f, f), BF16),
            pltpu.VMEM((f, f), BF16),
            pltpu.VMEM((n_t, 8, tl), jnp.int32),
            pltpu.VMEM((total, 128), jnp.int32),
            pltpu.VMEM((n_t, total, f), BF16),
            pltpu.VMEM((n_t, 8, total), F32),
            pltpu.VMEM((n_t, 8, tl), F32),
            pltpu.VMEM((n_t, 8, tl), F32),
            pltpu.SemaphoreType.DMA((4,)),
            pltpu.SemaphoreType.DMA((v // tile,)),
            pltpu.SemaphoreType.DMA((6, n_t)),
            pltpu.SemaphoreType.DMA((6, n_t)),
            pltpu.SemaphoreType.DMA((2, 6)),
            pltpu.SemaphoreType.DMA((2, 6)),
            pltpu.SemaphoreType.DMA((1 + v // tile, n_s, 3)),
            pltpu.SemaphoreType.DMA((1 + v // tile, n_s)),
        ],
        compiler_params=pltpu.CompilerParams(
            collective_id=0, has_side_effects=True, vmem_limit_bytes=60 * 1024 * 1024
        ),
    )(
        tokens, norm_gain.reshape(1, d), gate_w, up_w, down_w, final_gain.reshape(1, d), vocab_w,
        targets.reshape(1, tl), lengths,
    )
    return losses.reshape(tl)


def solution(mesh):
    return jax.shard_map(
        functools.partial(body, mesh.shape["tensor"], mesh.shape["dp"]),
        mesh=mesh,
        in_specs=(
            P(("dp", "tensor"), None),
            P(),
            P(None, "tensor"),
            P(None, "tensor"),
            P("tensor", None),
            P(),
            P("tensor", None),
            P(("dp", "tensor")),
            P("dp"),
        ),
        out_specs=P(("dp", "tensor")),
        check_vma=False,
    )
```

```python
import functools

import jax
import jax.numpy as jnp
from jax import lax
from jax.experimental import pallas as pl
from jax.experimental.pallas import tpu as pltpu
from jax.sharding import PartitionSpec as P

PACK_LEN = 128
EPS = 1e-06
SHRINK = 2.0**-27
GROW = 2.0**27
F32, BF16 = jnp.float32, jnp.bfloat16
NT = (((1,), (1,)), ((), ()))


def dot(a, b):
    return jnp.dot(a, b, preferred_element_type=F32)


def dot_nt(a, b):
    return lax.dot_general(a, b, NT, preferred_element_type=F32)


def diagonal(rows):
    shape = (rows, rows)
    return lax.broadcasted_iota(jnp.int32, shape, 0) == lax.broadcasted_iota(jnp.int32, shape, 1)


def to_column(row):
    n = row.shape[1]
    return jnp.sum(jnp.where(diagonal(n), row, jnp.zeros_like(row)), axis=1, keepdims=True)


def to_row(column):
    n = column.shape[0]
    return jnp.sum(jnp.where(diagonal(n), column, jnp.zeros_like(column)), axis=0, keepdims=True)


def kernel(
    n_t, n_s, tile,
    tok_in, ng, gate_in, up_in, down_in, fg, voc_in, tgt, lens,
    out,
    tok, sl, gu, dw, voc, xn, xg, sg, sgo, x2, cross, logit, w2, gram, glow, tg, tgc, hid, qs, sts, sta,
    local_sem, voc_sem, t_send, t_recv, r_send, r_recv, s_send, s_recv, far_sem,
):
    me = lax.axis_index("tensor")
    dp = lax.axis_index("dp")
    slot = lax.rem(dp, n_s)
    group = dp - slot
    _, tl, d = tok.shape
    rows = sl.shape[1]
    f = dw.shape[0]
    v = voc.shape[0]
    total = n_t * tl
    n_v = v // tile

    def local(i, src, dst):
        copy = pltpu.make_async_copy(src, dst, local_sem.at[i])
        copy.start()
        return copy

    own_rows = pl.ds(pl.multiple_of(slot * rows, rows), rows)
    own_tok = local(0, tok_in, tok.at[me])

    barrier = pltpu.get_barrier_semaphore()
    for k in range(1, n_t):
        pl.semaphore_signal(barrier, inc=1, device_id={"tensor": lax.rem(me + k, n_t)})
    n_z = n_s // 2
    z, core = slot // 2, lax.rem(slot, 2)
    sibling = 2 * z + 1 - core
    pl.semaphore_signal(barrier, inc=1, device_id={"dp": group + sibling})

    @pl.when(z > 0)
    def _():
        pl.semaphore_signal(barrier, inc=1, device_id={"dp": group + slot - 2})

    @pl.when(z < n_z - 1)
    def _():
        pl.semaphore_signal(barrier, inc=1, device_id={"dp": group + slot + 2})


    down_copy = local(1, down_in, dw)

    def voc_copy(c):
        part = pl.ds(pl.multiple_of(c * tile, tile), tile)
        return pltpu.make_async_copy(voc_in.at[part], voc.at[part], voc_sem.at[c])

    for c in range(n_v):
        voc_copy(c).start()
    gate_copy = local(2, gate_in, gu.at[:, pl.ds(0, f)])
    up_copy = local(3, up_in, gu.at[:, pl.ds(f, f)])
    tg[me] = jnp.broadcast_to(tgt[...], tg.shape[1:])
    beside = sum((z + n_z - q) // n_z + (2 * n_z - 1 - q - z) // n_z for q in (1,))
    pl.semaphore_wait(barrier, n_t + beside)

    def t_copy(kind, src, dst, k):
        return pltpu.make_async_remote_copy(
            src_ref=src, dst_ref=dst, send_sem=t_send.at[kind], recv_sem=t_recv.at[kind],
            device_id={"tensor": lax.rem(me + k, n_t)},
        )

    def piece(kind, j, count=1):
        part = pl.ds(pl.multiple_of(j * rows, rows), count * rows)
        if kind == 0:
            return gram.at[pl.ds(1, n_t - 1), part, :]
        return w2.at[pl.ds(1, n_t - 1), part, pl.ds((kind - 1) * tile, tile)]

    def entered(stage):
        for sign, sem in ((-1, 0), (1, 1)):
            ahead = (n_z - 1 - z) if sign < 0 else z

            def tell():
                @pl.when(jnp.logical_and(ahead >= 1, ahead <= n_z - 2))
                def _():
                    pl.semaphore_signal(far_sem.at[sem], inc=1, device_id={"dp": group + slot + 2 * sign})

            if stage == 0:
                @pl.when(ahead == 1)
                def _():
                    tell()
            else:
                @pl.when(ahead >= 2)
                def _():
                    pl.semaphore_wait(far_sem.at[sem], 1)
                    tell()

    inner = jnp.logical_and(z > 0, z < n_z - 1)

    def s_remote(ref, family, way, kind, landing, to):
        return pltpu.make_async_remote_copy(
            src_ref=ref, dst_ref=ref, send_sem=s_send.at[family, way], recv_sem=s_recv.at[kind, landing],
            device_id={"dp": group + to},
        )

    def s_copy(kind, j, way, to):
        return s_remote(piece(kind, j), min(kind, 1), way, kind, n_z if to is sibling else j // 2, to)

    n_far = 2 * max(0, n_z - 3)

    def s_ways(j, step, sign, act):
        if step == 0:
            for dist in range(3, n_z):
                for side in (-1, 1):
                    @pl.when(jnp.logical_and(z + side * dist >= 0, z + side * dist <= n_z - 1))
                    def _():
                        act(j, 3 + 2 * (dist - 3) + (side + 1) // 2, slot + 2 * side * dist)

            @pl.when(z > 0)
            def _():
                act(j, 0, slot - 2)

            @pl.when(z < n_z - 1)
            def _():
                act(j, 1, slot + 2)

            act(j, 2, sibling)
        else:
            if step == 1:
                @pl.when(inner)
                def _():
                    act(j, 3 + n_far + (sign + 1) // 2, slot - 2 * sign)

            act(j, 5 + n_far + j // 2, sibling)

    def s_own(kind):
        s_ways(slot, 0, 0, lambda j, way, to: s_copy(kind, j, way, to).start())

    def s_relay(kind, step, relays):
        for sign in (-1, 1):
            there = jnp.logical_and(z + sign * step >= 0, z + sign * step <= n_z - 1)
            if step == 1:
                there = jnp.logical_and(there, inner if relays else jnp.logical_not(inner))

            @pl.when(there)
            def _():
                j = slot + 2 * sign * step
                s_remote(piece(kind, j), min(kind, 1), 0, kind, j // 2, sibling).wait_recv()
                s_ways(j, step, sign, lambda j, way, to: s_copy(kind, j, way, to).start())

    def s_arrived(kind):
        every = piece(kind, 0, n_z)
        s_remote(every, 0, 0, kind, n_z, sibling).wait_recv()

    def s_sent(family):
        def wait(j, way, to):
            part = pl.ds(pl.multiple_of(j * rows, rows), rows)
            ref = (w2 if family else gram).at[pl.ds(1, n_t - 1), part, :]
            s_remote(ref, family, way, family, n_z, to).wait_send()

        s_ways(slot, 0, 0, wait)
        for step in range(1, n_z):
            for sign in (-1, 1):
                @pl.when(jnp.logical_and(z + sign * step >= 0, z + sign * step <= n_z - 1))
                def _():
                    s_ways(slot + 2 * sign * step, step, sign, wait)

    def block(k):
        return lax.rem(me + k, n_t)

    def t_start(kind, src, dst, buf):
        for k in range(1, n_t):
            t_copy(kind, src(k), dst(k), k).start()
        others = buf.at[pl.ds(1, n_t - 1)]
        return t_copy(kind, others, others, 1)

    relayed = n_t == 4
    if relayed:
        y, x = me // 2, lax.rem(me, 2)
        x_near, y_near, far = 2 * y + 1 - x, 2 * (1 - y) + x, 2 * (1 - y) + 1 - x

    def half(ref, h):
        return ref.at[:, pl.ds(h * (d // 2), d // 2)]

    def r_copies(kind, src, buf, place):
        plan = (
            (half(src, 0), me, 0, x_near), (half(src, 1), me, 1, x_near),
            (half(src, 1), me, 1, y_near), (half(src, 0), me, 0, y_near),
            (half(buf.at[place(y_near, me)], 1), y_near, 1, x_near),
            (half(buf.at[place(x_near, me)], 0), x_near, 0, y_near),
        )
        def remote(src, dst, group_index, to):
            return pltpu.make_async_remote_copy(
                src_ref=src, dst_ref=dst, send_sem=r_send.at[kind], recv_sem=r_recv.at[kind, group_index],
                device_id={"tensor": to},
            )

        copies = [
            remote(part, half(buf.at[place(owner, to)], h), (0, 2, 1, 2, 3, 3)[i], to)
            for i, (part, owner, h, to) in enumerate(plan)
        ]
        one, three = buf.at[0], buf.at[pl.ds(0, 3)]
        return copies, [remote(one, one, i, x_near) for i in (2, 3)], remote(three, three, 0, x_near)

    def r_start(copies):
        for i in (0, 2, 1, 3):
            copies[0][i].start()

    def r_pass(copies):
        copies[0][0].wait_recv()
        copies[0][5].start()
        copies[0][2].wait_recv()
        copies[0][4].start()

    down_rows = down_in.at[own_rows]
    if relayed:
        sl_copies = r_copies(0, down_rows, sl, lambda owner, to: lax.rem(owner - to + n_t, n_t))
        tok_copies = r_copies(1, tok_in, tok, lambda owner, to: owner)
        r_start(sl_copies)
    else:
        sl_copies = t_start(4, lambda k: down_rows, lambda k: sl.at[n_t - k], sl)
        tok_copies = t_start(5, lambda k: tok_in, lambda k: tok.at[me], tok)

    def token_block(index):
        part = pl.ds(pl.multiple_of(index * tl, tl), tl)
        x = tok[index].astype(F32)
        square = jnp.sum(x * x, axis=1, keepdims=True)
        x2[part, :] = jnp.broadcast_to(square, (tl, x2.shape[1]))
        xn[part, :] = (x * lax.rsqrt(square * (1.0 / d) + EPS) * ng[...]).astype(BF16)
        xg[part, :] = (x * (fg[...] * SHRINK)).astype(BF16)

    if n_z > 3:
        entered(0)
    tg_copies = t_start(0, lambda k: tg.at[me], lambda k: tg.at[me], tg)
    own_tok.wait()
    token_block(me)
    down_copy.wait()
    sgo[...] = (dw[...].astype(F32) * (fg[...] * SHRINK)).astype(BF16)

    def own_w2(c):
        voc_copy(c).wait()
        part = pl.ds(c * tile, tile)
        w2[0, :, part] = dot_nt(sgo[...], voc[part, :]).astype(BF16)

    own_w2(0)
    if relayed:
        r_pass(sl_copies)
        r_start(tok_copies)
    own_w2(1)
    if n_z > 3:
        entered(1)
    for c in range(2, n_v):
        own_w2(c)
    own_gram = dot_nt(dw[...], dw[...])
    own_high = own_gram.astype(BF16)
    gram[0] = own_high
    glow[...] = (own_gram - own_high.astype(F32)).astype(BF16)

    if relayed:
        for copy in sl_copies[1]:
            copy.wait_recv()
    else:
        sl_copies.wait_recv()
    raw = sl[pl.ds(1, n_t - 1)].reshape((n_t - 1) * rows, d)
    gram[pl.ds(1, n_t - 1), own_rows, :] = dot_nt(raw, dw[...]).astype(BF16).reshape(n_t - 1, rows, f)
    s_own(0)
    sg[...] = (raw.astype(F32) * (fg[...] * SHRINK)).astype(BF16)
    for c in range(n_v):
        part = pl.ds(c * tile, tile)
        w2[pl.ds(1, n_t - 1), own_rows, part] = dot_nt(sg[...], voc[part, :]).astype(BF16).reshape(n_t - 1, rows, tile)
        s_own(1 + c)
        if relayed and c == n_v // 2:
            r_pass(tok_copies)

    kinds = range(n_v + 1)

    def gate_up():
        gate_copy.wait()
        up_copy.wait()
        both = dot(xn[...], gu[...])
        gate, up = both[:, :f], both[:, f:]
        hid[me] = (gate / (1.0 + jnp.exp(-gate)) * up).astype(BF16)
        return t_start(1, lambda k: hid.at[me], lambda k: hid.at[me], hid)

    def token_logits(c):
        part = pl.ds(c * tile, tile)
        logit[:, part] = dot_nt(xg[...], voc[part, :])

    steps = range(1, n_z)
    pairs = [(kind, step) for kind in kinds for step in steps]
    inner_order = [(kind, 1) for kind in kinds]
    end_order = sorted(pairs, key=lambda e: (e[0] > 0, e[0] + 2 * e[1]))

    def relay(count, end_count):
        for order, n, relays in ((inner_order, count, True), (end_order, end_count, False)):
            for kind, step in order[:n]:
                s_relay(kind, step, relays)
            del order[:n]

    if relayed:
        tok_copies[1][0].wait_recv()
        token_block(x_near)
        token_block(y_near)
        relay(3, 0)
        tok_copies[1][1].wait_recv()
        token_block(far)
    else:
        tok_copies.wait_recv()
        for k in range(1, n_t):
            token_block(lax.rem(me + n_t - k, n_t))
        relay(3, 0)
    h_copies = gate_up()
    relay(1, 0)
    cross[...] = dot_nt(tok[...].reshape(total, d), dw[...])
    relay(0, 0)
    token_logits(0)
    relay(0, 0)
    for c in range(1, n_v - 1):
        token_logits(c)
    relay(0, 3)
    tg_copies.wait_recv()
    for t in range(n_t):
        tgc[pl.ds(t * tl, tl), :] = jnp.broadcast_to(to_column(tg[t][0:1, :]), (tl, tgc.shape[1]))
    h_copies.wait_recv()
    for kind, step in pairs:
        if kind == 0 and (kind, step) in inner_order:
            s_relay(kind, step, True)
            inner_order.remove((kind, step))
        if kind == 0 and (kind, step) in end_order:
            s_relay(kind, step, False)
            end_order.remove((kind, step))
    s_arrived(0)
    hidden = jnp.concatenate([hid[block(k)] for k in range(n_t)], axis=1)
    pulled = dot(hidden, gram[...].reshape(n_t * f, f)) + dot(hid[me], glow[...])
    share = jnp.sum(hid[me].astype(F32) * (2.0 * cross[...] + pulled), axis=1, keepdims=True)
    qs[me] = jnp.broadcast_to(to_row(share), qs.shape[1:])
    q_copies = t_start(2, lambda k: qs.at[me], lambda k: qs.at[me], qs)

    relay(len(inner_order), 0)
    token_logits(n_v - 1)
    relay(0, len(end_order))
    for c in range(n_v):
        s_arrived(1 + c)
        part = pl.ds(c * tile, tile)
        logit[:, part] += dot(hidden, w2[:, :, part].reshape(n_t * f, tile))

    q_copies.wait_recv()
    pulls = qs[0, 0:1, :]
    for t in range(1, n_t):
        pulls = pulls + qs[t, 0:1, :]
    square = jnp.maximum(x2[:, 0:1] + to_column(pulls), 0.0)
    x2[...] = jnp.broadcast_to(lax.rsqrt(square * (1.0 / d) + EPS) * GROW, x2.shape)

    @pl.loop(0, n_t, unroll=min(n_t, 4))
    def _(t):
        part = pl.ds(pl.multiple_of(t * tl, tl), tl)
        scaled = logit[part, :] * x2[part, 0:1]
        top = jnp.max(scaled, axis=1, keepdims=True)
        mass = jnp.sum(jnp.exp(scaled - top), axis=1, keepdims=True)
        columns = lax.broadcasted_iota(jnp.int32, (tl, v), 1) + me * v
        hit = jnp.sum(jnp.where(columns == tgc[part, 0:1], scaled, 0.0), axis=1, keepdims=True)
        sts[t, 0:1, :] = to_row(top)
        sts[t, 1:2, :] = to_row(mass)
        sts[t, 2:3, :] = to_row(hit)

    end = t_start(3, lambda k: sts.at[block(k)], lambda k: sta.at[me], sta)
    sta[me] = sts[me]
    positions = me * tl + lax.broadcasted_iota(jnp.int32, (1, tl), 1)
    packs = positions // PACK_LEN
    limits = jnp.zeros((1, tl), jnp.int32)
    for i in range(lens.shape[0]):
        limits = jnp.where(packs == i, lens[i], limits)
    end.wait_recv()
    stats = [sta[t] for t in range(n_t)]
    top = stats[0][0:1, :]
    for s in stats[1:]:
        top = jnp.maximum(top, s[0:1, :])
    mass = sum(s[1:2, :] * jnp.exp(s[0:1, :] - top) for s in stats)
    hit = sum(s[2:3, :] for s in stats)
    out[...] = jnp.where(positions - packs * PACK_LEN < limits, top + jnp.log(mass) - hit, 0.0)

    for copy in (sl_copies, tok_copies):
        (copy[2] if relayed else copy).wait_send()
    for copy in (tg_copies, h_copies, q_copies, end):
        copy.wait_send()
    for family in (0, 1):
        s_sent(family)


def body(n_t, n_dp, tokens, norm_gain, gate_w, up_w, down_w, final_gain, vocab_w, targets, lengths):
    tl, d = tokens.shape
    f = down_w.shape[0]
    v = vocab_w.shape[0]
    n_s = min(n_dp, f // 16)
    n_z = n_s // 2
    rows = f // n_s
    total = n_t * tl
    tile = next(size for size in (384, 256, 128) if v % size == 0)
    vmem = pl.BlockSpec(memory_space=pltpu.VMEM)
    hbm = pl.BlockSpec(memory_space=pl.ANY)
    losses = pl.pallas_call(
        functools.partial(kernel, n_t, n_s, tile),
        out_shape=jax.ShapeDtypeStruct((1, tl), F32),
        in_specs=[hbm, vmem, hbm, hbm, hbm, vmem, hbm, vmem, pl.BlockSpec(memory_space=pltpu.SMEM)],
        out_specs=vmem,
        scratch_shapes=[
            pltpu.VMEM((n_t, tl, d), BF16),
            pltpu.VMEM((n_t, rows, d), BF16),
            pltpu.VMEM((d, 2 * f), BF16),
            pltpu.VMEM((f, d), BF16),
            pltpu.VMEM((v, d), BF16),
            pltpu.VMEM((total, d), BF16),
            pltpu.VMEM((total, d), BF16),
            pltpu.VMEM(((n_t - 1) * rows, d), BF16),
            pltpu.VMEM((f, d), BF16),
            pltpu.VMEM((total, 128), F32),
            pltpu.VMEM((total, f), F32),
            pltpu.VMEM((total, v), F32),
            pltpu.VMEM((n_t, f, v), BF16),
            pltpu.VMEM((n_t, f, f), BF16),
            pltpu.VMEM((f, f), BF16),
            pltpu.VMEM((n_t, 8, tl), jnp.int32),
            pltpu.VMEM((total, 128), jnp.int32),
            pltpu.VMEM((n_t, total, f), BF16),
            pltpu.VMEM((n_t, 8, total), F32),
            pltpu.VMEM((n_t, 8, tl), F32),
            pltpu.VMEM((n_t, 8, tl), F32),
            pltpu.SemaphoreType.DMA((4,)),
            pltpu.SemaphoreType.DMA((v // tile,)),
            pltpu.SemaphoreType.DMA((4 if n_t == 4 else 6,)),
            pltpu.SemaphoreType.DMA((4 if n_t == 4 else 6,)),
            pltpu.SemaphoreType.DMA((2,)),
            pltpu.SemaphoreType.DMA((2, 4)),
            pltpu.SemaphoreType.DMA((2, 5 + 2 * max(0, n_z - 3) + n_z)),
            pltpu.SemaphoreType.DMA((1 + v // tile, n_z + 1)),
            pltpu.SemaphoreType.REGULAR((2,)),
        ],
        compiler_params=pltpu.CompilerParams(
            collective_id=0, has_side_effects=True, vmem_limit_bytes=60 * 1024 * 1024
        ),
    )(
        tokens, norm_gain.reshape(1, d), gate_w, up_w, down_w, final_gain.reshape(1, d), vocab_w,
        targets.reshape(1, tl), lengths,
    )
    return losses.reshape(tl)


def solution(mesh):
    return jax.shard_map(
        functools.partial(body, mesh.shape["tensor"], mesh.shape["dp"]),
        mesh=mesh,
        in_specs=(
            P(("dp", "tensor"), None),
            P(),
            P(None, "tensor"),
            P(None, "tensor"),
            P("tensor", None),
            P(),
            P("tensor", None),
            P(("dp", "tensor")),
            P("dp"),
        ),
        out_specs=P(("dp", "tensor")),
        check_vma=False,
    )
```

```python
import functools

import jax
import jax.numpy as jnp
from jax import lax
from jax.experimental import pallas as pl
from jax.experimental.pallas import tpu as pltpu
from jax.sharding import PartitionSpec as P

PACK_LEN = 128
EPS = 1e-06
SHRINK = 2.0**-27
GROW = 2.0**27
F32, BF16 = jnp.float32, jnp.bfloat16
NT = (((1,), (1,)), ((), ()))


def dot(a, b):
    return jnp.dot(a, b, preferred_element_type=F32)


def dot_nt(a, b):
    return lax.dot_general(a, b, NT, preferred_element_type=F32)


def diagonal(rows):
    shape = (rows, rows)
    return lax.broadcasted_iota(jnp.int32, shape, 0) == lax.broadcasted_iota(jnp.int32, shape, 1)


def to_column(row):
    n = row.shape[1]
    return jnp.sum(jnp.where(diagonal(n), row, jnp.zeros_like(row)), axis=1, keepdims=True)


def to_row(column):
    n = column.shape[0]
    return jnp.sum(jnp.where(diagonal(n), column, jnp.zeros_like(column)), axis=0, keepdims=True)


def kernel(
    n_t, n_s, tile,
    tok_in, ng, gate_in, up_in, down_in, fg, voc_in, tgt, lens,
    out,
    tok, sl, gu, dw, voc, xn, xg, sg, sgo, x2, cross, logit, w2, gram, glow, tg, tgc, hid, qs, sts, sta,
    local_sem, voc_sem, t_send, t_recv, r_send, r_recv, s_send, s_recv, far_sem,
):
    me = lax.axis_index("tensor")
    dp = lax.axis_index("dp")
    slot = lax.rem(dp, n_s)
    group = dp - slot
    _, tl, d = tok.shape
    rows = sl.shape[1]
    f = dw.shape[0]
    v = voc.shape[0]
    total = n_t * tl
    n_v = v // tile

    def local(i, src, dst):
        copy = pltpu.make_async_copy(src, dst, local_sem.at[i])
        copy.start()
        return copy

    own_rows = pl.ds(pl.multiple_of(slot * rows, rows), rows)
    own_tok = local(0, tok_in, tok.at[me])

    barrier = pltpu.get_barrier_semaphore()
    for k in range(1, n_t):
        pl.semaphore_signal(barrier, inc=1, device_id={"tensor": lax.rem(me + k, n_t)})
    n_z = n_s // 2
    z, core = slot // 2, lax.rem(slot, 2)
    sibling = 2 * z + 1 - core
    pl.semaphore_signal(barrier, inc=1, device_id={"dp": group + sibling})

    @pl.when(z > 0)
    def _():
        pl.semaphore_signal(barrier, inc=1, device_id={"dp": group + slot - 2})

    @pl.when(z < n_z - 1)
    def _():
        pl.semaphore_signal(barrier, inc=1, device_id={"dp": group + slot + 2})


    down_copy = local(1, down_in, dw)

    def voc_copy(c):
        part = pl.ds(pl.multiple_of(c * tile, tile), tile)
        return pltpu.make_async_copy(voc_in.at[part], voc.at[part], voc_sem.at[c])

    for c in range(n_v):
        voc_copy(c).start()
    gate_copy = local(2, gate_in, gu.at[:, pl.ds(0, f)])
    up_copy = local(3, up_in, gu.at[:, pl.ds(f, f)])
    tg[me] = jnp.broadcast_to(tgt[...], tg.shape[1:])
    beside = sum((z + n_z - q) // n_z + (2 * n_z - 1 - q - z) // n_z for q in (1,))
    pl.semaphore_wait(barrier, n_t + beside)

    def t_copy(kind, src, dst, k):
        return pltpu.make_async_remote_copy(
            src_ref=src, dst_ref=dst, send_sem=t_send.at[kind], recv_sem=t_recv.at[kind],
            device_id={"tensor": lax.rem(me + k, n_t)},
        )

    def piece(kind, j, count=1):
        part = pl.ds(pl.multiple_of(j * rows, rows), count * rows)
        if kind == 0:
            return gram.at[pl.ds(1, n_t - 1), part, :]
        return w2.at[pl.ds(1, n_t - 1), part, pl.ds((kind - 1) * tile, tile)]

    def entered(stage):
        for sign, sem in ((-1, 0), (1, 1)):
            ahead = (n_z - 1 - z) if sign < 0 else z

            def tell():
                @pl.when(jnp.logical_and(ahead >= 1, ahead <= n_z - 2))
                def _():
                    pl.semaphore_signal(far_sem.at[sem], inc=1, device_id={"dp": group + slot + 2 * sign})

            if stage == 0:
                @pl.when(ahead == 1)
                def _():
                    tell()
            else:
                @pl.when(ahead >= 2)
                def _():
                    pl.semaphore_wait(far_sem.at[sem], 1)
                    tell()

    inner = jnp.logical_and(z > 0, z < n_z - 1)

    def s_remote(ref, family, way, kind, landing, to):
        return pltpu.make_async_remote_copy(
            src_ref=ref, dst_ref=ref, send_sem=s_send.at[family, way], recv_sem=s_recv.at[kind, landing],
            device_id={"dp": group + to},
        )

    def s_copy(kind, j, way, to):
        return s_remote(piece(kind, j), min(kind, 1), way, kind, n_z if to is sibling else j // 2, to)

    n_far = 2 * max(0, n_z - 3)

    def s_ways(j, step, sign, act):
        if step == 0:
            for dist in range(3, n_z):
                for side in (-1, 1):
                    @pl.when(jnp.logical_and(z + side * dist >= 0, z + side * dist <= n_z - 1))
                    def _():
                        act(j, 3 + 2 * (dist - 3) + (side + 1) // 2, slot + 2 * side * dist)

            @pl.when(z > 0)
            def _():
                act(j, 0, slot - 2)

            @pl.when(z < n_z - 1)
            def _():
                act(j, 1, slot + 2)

            act(j, 2, sibling)
        else:
            if step == 1:
                @pl.when(inner)
                def _():
                    act(j, 3 + n_far + (sign + 1) // 2, slot - 2 * sign)

            act(j, 5 + n_far + j // 2, sibling)

    def s_own(kind):
        s_ways(slot, 0, 0, lambda j, way, to: s_copy(kind, j, way, to).start())

    def s_relay(kind, step, relays):
        for sign in (-1, 1):
            there = jnp.logical_and(z + sign * step >= 0, z + sign * step <= n_z - 1)
            if step == 1:
                there = jnp.logical_and(there, inner if relays else jnp.logical_not(inner))

            @pl.when(there)
            def _():
                j = slot + 2 * sign * step
                s_remote(piece(kind, j), min(kind, 1), 0, kind, j // 2, sibling).wait_recv()
                s_ways(j, step, sign, lambda j, way, to: s_copy(kind, j, way, to).start())

    def s_arrived(kind):
        every = piece(kind, 0, n_z)
        s_remote(every, 0, 0, kind, n_z, sibling).wait_recv()

    def s_sent(family):
        def wait(j, way, to):
            part = pl.ds(pl.multiple_of(j * rows, rows), rows)
            ref = (w2 if family else gram).at[pl.ds(1, n_t - 1), part, :]
            s_remote(ref, family, way, family, n_z, to).wait_send()

        s_ways(slot, 0, 0, wait)
        for step in range(1, n_z):
            for sign in (-1, 1):
                @pl.when(jnp.logical_and(z + sign * step >= 0, z + sign * step <= n_z - 1))
                def _():
                    s_ways(slot + 2 * sign * step, step, sign, wait)

    def block(k):
        return lax.rem(me + k, n_t)

    def t_start(kind, src, dst, buf):
        for k in range(1, n_t):
            t_copy(kind, src(k), dst(k), k).start()
        others = buf.at[pl.ds(1, n_t - 1)]
        return t_copy(kind, others, others, 1)

    relayed = n_t == 4
    if relayed:
        y, x = me // 2, lax.rem(me, 2)
        x_near, y_near, far = 2 * y + 1 - x, 2 * (1 - y) + x, 2 * (1 - y) + 1 - x

    def half(ref, h):
        return ref.at[:, pl.ds(h * (d // 2), d // 2)]

    def r_copies(kind, src, buf, place):
        plan = (
            (half(src, 0), me, 0, x_near), (half(src, 1), me, 1, x_near),
            (half(src, 1), me, 1, y_near), (half(src, 0), me, 0, y_near),
            (half(buf.at[place(y_near, me)], 1), y_near, 1, x_near),
            (half(buf.at[place(x_near, me)], 0), x_near, 0, y_near),
        )
        def remote(src, dst, group_index, to):
            return pltpu.make_async_remote_copy(
                src_ref=src, dst_ref=dst, send_sem=r_send.at[kind], recv_sem=r_recv.at[kind, group_index],
                device_id={"tensor": to},
            )

        copies = [
            remote(part, half(buf.at[place(owner, to)], h), (0, 2, 1, 2, 3, 3)[i], to)
            for i, (part, owner, h, to) in enumerate(plan)
        ]
        one, three = buf.at[0], buf.at[pl.ds(0, 3)]
        return copies, [remote(one, one, i, x_near) for i in (2, 3)], remote(three, three, 0, x_near)

    def r_start(copies):
        for i in (0, 2, 1, 3):
            copies[0][i].start()

    def r_pass(copies):
        copies[0][0].wait_recv()
        copies[0][5].start()
        copies[0][2].wait_recv()
        copies[0][4].start()

    down_rows = down_in.at[own_rows]
    if relayed:
        sl_copies = r_copies(0, down_rows, sl, lambda owner, to: lax.rem(owner - to + n_t, n_t))
        tok_copies = r_copies(1, tok_in, tok, lambda owner, to: owner)
        r_start(sl_copies)
    else:
        sl_copies = t_start(4, lambda k: down_rows, lambda k: sl.at[n_t - k], sl)
        tok_copies = t_start(5, lambda k: tok_in, lambda k: tok.at[me], tok)

    def token_block(index):
        part = pl.ds(pl.multiple_of(index * tl, tl), tl)
        x = tok[index].astype(F32)
        square = jnp.sum(x * x, axis=1, keepdims=True)
        x2[part, :] = jnp.broadcast_to(square, (tl, x2.shape[1]))
        xn[part, :] = (x * lax.rsqrt(square * (1.0 / d) + EPS) * ng[...]).astype(BF16)
        xg[part, :] = (x * (fg[...] * SHRINK)).astype(BF16)

    if n_z > 3:
        entered(0)
    tg_copies = t_start(0, lambda k: tg.at[me], lambda k: tg.at[me], tg)
    own_tok.wait()
    token_block(me)
    down_copy.wait()
    sgo[...] = (dw[...].astype(F32) * (fg[...] * SHRINK)).astype(BF16)

    def own_w2(c):
        voc_copy(c).wait()
        part = pl.ds(c * tile, tile)
        w2[0, :, part] = dot_nt(sgo[...], voc[part, :]).astype(BF16)

    own_w2(0)
    if relayed:
        r_pass(sl_copies)
        r_start(tok_copies)
    own_w2(1)
    if n_z > 3:
        entered(1)
    for c in range(2, n_v):
        own_w2(c)
    own_gram = dot_nt(dw[...], dw[...])
    own_high = own_gram.astype(BF16)
    gram[0] = own_high
    glow[...] = (own_gram - own_high.astype(F32)).astype(BF16)

    if relayed:
        for copy in sl_copies[1]:
            copy.wait_recv()
    else:
        sl_copies.wait_recv()
    raw = sl[pl.ds(1, n_t - 1)].reshape((n_t - 1) * rows, d)
    gram[pl.ds(1, n_t - 1), own_rows, :] = dot_nt(raw, dw[...]).astype(BF16).reshape(n_t - 1, rows, f)
    s_own(0)
    sg[...] = (raw.astype(F32) * (fg[...] * SHRINK)).astype(BF16)
    for c in range(n_v):
        part = pl.ds(c * tile, tile)
        w2[pl.ds(1, n_t - 1), own_rows, part] = dot_nt(sg[...], voc[part, :]).astype(BF16).reshape(n_t - 1, rows, tile)
        s_own(1 + c)
        if relayed and c == 0:
            r_pass(tok_copies)

    kinds = range(n_v + 1)

    def gate_up():
        gate_copy.wait()
        up_copy.wait()
        both = dot(xn[...], gu[...])
        gate, up = both[:, :f], both[:, f:]
        hid[me] = (gate / (1.0 + jnp.exp(-gate)) * up).astype(BF16)
        return t_start(1, lambda k: hid.at[me], lambda k: hid.at[me], hid)

    def token_logits(c):
        part = pl.ds(c * tile, tile)
        logit[:, part] = dot_nt(xg[...], voc[part, :])

    steps = range(1, n_z)
    pairs = [(kind, step) for kind in kinds for step in steps]
    inner_order = [(kind, 1) for kind in kinds]
    end_order = sorted(pairs, key=lambda e: (e[0] > 0, e[0] + 2 * e[1]))

    def relay(count, end_count):
        for order, n, relays in ((inner_order, count, True), (end_order, end_count, False)):
            for kind, step in order[:n]:
                s_relay(kind, step, relays)
            del order[:n]

    if relayed:
        tok_copies[1][0].wait_recv()
        token_block(x_near)
        token_block(y_near)
        relay(3, 0)
        tok_copies[1][1].wait_recv()
        token_block(far)
    else:
        tok_copies.wait_recv()
        for k in range(1, n_t):
            token_block(lax.rem(me + n_t - k, n_t))
        relay(3, 0)
    h_copies = gate_up()
    relay(1, 0)
    cross[...] = dot_nt(tok[...].reshape(total, d), dw[...])
    relay(0, 0)
    token_logits(0)
    relay(0, 0)
    for c in range(1, n_v - 1):
        token_logits(c)
    relay(0, 3)
    tg_copies.wait_recv()
    for t in range(n_t):
        tgc[pl.ds(t * tl, tl), :] = jnp.broadcast_to(to_column(tg[t][0:1, :]), (tl, tgc.shape[1]))
    h_copies.wait_recv()
    for kind, step in pairs:
        if kind == 0 and (kind, step) in inner_order:
            s_relay(kind, step, True)
            inner_order.remove((kind, step))
        if kind == 0 and (kind, step) in end_order:
            s_relay(kind, step, False)
            end_order.remove((kind, step))
    s_arrived(0)
    hidden = jnp.concatenate([hid[block(k)] for k in range(n_t)], axis=1)
    pulled = dot(hidden, gram[...].reshape(n_t * f, f)) + dot(hid[me], glow[...])
    share = jnp.sum(hid[me].astype(F32) * (2.0 * cross[...] + pulled), axis=1, keepdims=True)
    qs[me] = jnp.broadcast_to(to_row(share), qs.shape[1:])
    q_copies = t_start(2, lambda k: qs.at[me], lambda k: qs.at[me], qs)

    relay(len(inner_order), 0)
    token_logits(n_v - 1)
    relay(0, len(end_order))
    for c in range(n_v):
        s_arrived(1 + c)
        part = pl.ds(c * tile, tile)
        logit[:, part] += dot(hidden, w2[:, :, part].reshape(n_t * f, tile))

    @pl.loop(0, n_t, unroll=min(n_t, 4))
    def _(t):
        part = pl.ds(pl.multiple_of(t * tl, tl), tl)
        raw_logit = logit[part, :]
        top = jnp.max(raw_logit, axis=1, keepdims=True)
        columns = lax.broadcasted_iota(jnp.int32, (tl, v), 1) + me * v
        hit = jnp.sum(jnp.where(columns == tgc[part, 0:1], raw_logit, 0.0), axis=1, keepdims=True)
        logit[part, :] = raw_logit - top
        sts[t, 0:1, :] = to_row(top)
        sts[t, 2:3, :] = to_row(hit)

    q_copies.wait_recv()
    pulls = qs[0, 0:1, :]
    for t in range(1, n_t):
        pulls = pulls + qs[t, 0:1, :]

    square = jnp.maximum(x2[:, 0:1] + to_column(pulls), 0.0)
    scale = lax.rsqrt(square * (1.0 / d) + EPS) * GROW
    x2[...] = jnp.broadcast_to(scale, x2.shape)

    @pl.loop(0, n_t, unroll=min(n_t, 4))
    def _(t):
        part = pl.ds(pl.multiple_of(t * tl, tl), tl)
        grow = x2[part, 0:1]
        mass = jnp.sum(jnp.exp(logit[part, :] * grow), axis=1, keepdims=True)
        row = to_row(grow)
        sts[t, 0:1, :] = sts[t, 0:1, :] * row
        sts[t, 1:2, :] = to_row(mass)
        sts[t, 2:3, :] = sts[t, 2:3, :] * row

    end = t_start(3, lambda k: sts.at[block(k)], lambda k: sta.at[me], sta)
    sta[me] = sts[me]
    positions = me * tl + lax.broadcasted_iota(jnp.int32, (1, tl), 1)
    packs = positions // PACK_LEN
    limits = jnp.zeros((1, tl), jnp.int32)
    for i in range(lens.shape[0]):
        limits = jnp.where(packs == i, lens[i], limits)
    end.wait_recv()
    stats = [sta[t] for t in range(n_t)]
    top = stats[0][0:1, :]
    for s in stats[1:]:
        top = jnp.maximum(top, s[0:1, :])
    mass = sum(s[1:2, :] * jnp.exp(s[0:1, :] - top) for s in stats)
    hit = sum(s[2:3, :] for s in stats)
    out[...] = jnp.where(positions - packs * PACK_LEN < limits, top + jnp.log(mass) - hit, 0.0)

    for copy in (sl_copies, tok_copies):
        (copy[2] if relayed else copy).wait_send()
    for copy in (tg_copies, h_copies, q_copies, end):
        copy.wait_send()
    for family in (0, 1):
        s_sent(family)


def body(n_t, n_dp, tokens, norm_gain, gate_w, up_w, down_w, final_gain, vocab_w, targets, lengths):
    tl, d = tokens.shape
    f = down_w.shape[0]
    v = vocab_w.shape[0]
    n_s = min(n_dp, f // 16)
    n_z = n_s // 2
    rows = f // n_s
    total = n_t * tl
    tile = next(size for size in (384, 256, 128) if v % size == 0)
    vmem = pl.BlockSpec(memory_space=pltpu.VMEM)
    hbm = pl.BlockSpec(memory_space=pl.ANY)
    losses = pl.pallas_call(
        functools.partial(kernel, n_t, n_s, tile),
        out_shape=jax.ShapeDtypeStruct((1, tl), F32),
        in_specs=[hbm, vmem, hbm, hbm, hbm, vmem, hbm, vmem, pl.BlockSpec(memory_space=pltpu.SMEM)],
        out_specs=vmem,
        scratch_shapes=[
            pltpu.VMEM((n_t, tl, d), BF16),
            pltpu.VMEM((n_t, rows, d), BF16),
            pltpu.VMEM((d, 2 * f), BF16),
            pltpu.VMEM((f, d), BF16),
            pltpu.VMEM((v, d), BF16),
            pltpu.VMEM((total, d), BF16),
            pltpu.VMEM((total, d), BF16),
            pltpu.VMEM(((n_t - 1) * rows, d), BF16),
            pltpu.VMEM((f, d), BF16),
            pltpu.VMEM((total, 128), F32),
            pltpu.VMEM((total, f), F32),
            pltpu.VMEM((total, v), F32),
            pltpu.VMEM((n_t, f, v), BF16),
            pltpu.VMEM((n_t, f, f), BF16),
            pltpu.VMEM((f, f), BF16),
            pltpu.VMEM((n_t, 8, tl), jnp.int32),
            pltpu.VMEM((total, 128), jnp.int32),
            pltpu.VMEM((n_t, total, f), BF16),
            pltpu.VMEM((n_t, 8, total), F32),
            pltpu.VMEM((n_t, 8, tl), F32),
            pltpu.VMEM((n_t, 8, tl), F32),
            pltpu.SemaphoreType.DMA((4,)),
            pltpu.SemaphoreType.DMA((v // tile,)),
            pltpu.SemaphoreType.DMA((4 if n_t == 4 else 6,)),
            pltpu.SemaphoreType.DMA((4 if n_t == 4 else 6,)),
            pltpu.SemaphoreType.DMA((2,)),
            pltpu.SemaphoreType.DMA((2, 4)),
            pltpu.SemaphoreType.DMA((2, 5 + 2 * max(0, n_z - 3) + n_z)),
            pltpu.SemaphoreType.DMA((1 + v // tile, n_z + 1)),
            pltpu.SemaphoreType.REGULAR((2,)),
        ],
        compiler_params=pltpu.CompilerParams(
            collective_id=0, has_side_effects=True, vmem_limit_bytes=60 * 1024 * 1024
        ),
    )(
        tokens, norm_gain.reshape(1, d), gate_w, up_w, down_w, final_gain.reshape(1, d), vocab_w,
        targets.reshape(1, tl), lengths,
    )
    return losses.reshape(tl)


def solution(mesh):
    return jax.shard_map(
        functools.partial(body, mesh.shape["tensor"], mesh.shape["dp"]),
        mesh=mesh,
        in_specs=(
            P(("dp", "tensor"), None),
            P(),
            P(None, "tensor"),
            P(None, "tensor"),
            P("tensor", None),
            P(),
            P("tensor", None),
            P(("dp", "tensor")),
            P("dp"),
        ),
        out_specs=P(("dp", "tensor")),
        check_vma=False,
    )
```

```python
import functools

import jax
import jax.numpy as jnp
from jax import lax
from jax.experimental import pallas as pl
from jax.experimental.pallas import tpu as pltpu
from jax.sharding import PartitionSpec as P

PACK_LEN = 128
EPS = 1e-06
SHRINK = 2.0**-27
GROW = 2.0**27
F32, BF16 = jnp.float32, jnp.bfloat16
NT = (((1,), (1,)), ((), ()))


def dot(a, b):
    return jnp.dot(a, b, preferred_element_type=F32)


def dot_nt(a, b):
    return lax.dot_general(a, b, NT, preferred_element_type=F32)


def diagonal(rows):
    shape = (rows, rows)
    return lax.broadcasted_iota(jnp.int32, shape, 0) == lax.broadcasted_iota(jnp.int32, shape, 1)


def to_column(row):
    n = row.shape[1]
    return jnp.sum(jnp.where(diagonal(n), row, jnp.zeros_like(row)), axis=1, keepdims=True)


def to_row(column):
    n = column.shape[0]
    return jnp.sum(jnp.where(diagonal(n), column, jnp.zeros_like(column)), axis=0, keepdims=True)


def kernel(
    n_t, n_s, tile,
    tok_in, ng, gate_in, up_in, down_in, fg, voc_in, tgt, lens,
    out,
    tok, sl, gu, dw, voc, xn, xg, sg, sgo, x2, cross, logit, w2, gram, glow, tg, tgc, hid, qs, sts, sta,
    local_sem, voc_sem, t_send, t_recv, r_send, r_recv, s_send, s_recv, far_sem,
):
    me = lax.axis_index("tensor")
    dp = lax.axis_index("dp")
    slot = lax.rem(dp, n_s)
    group = dp - slot
    _, tl, d = tok.shape
    rows = sl.shape[1]
    f = dw.shape[0]
    v = voc.shape[0]
    total = n_t * tl
    n_v = v // tile

    def local(i, src, dst):
        copy = pltpu.make_async_copy(src, dst, local_sem.at[i])
        copy.start()
        return copy

    own_rows = pl.ds(pl.multiple_of(slot * rows, rows), rows)
    own_tok = local(0, tok_in, tok.at[me])

    barrier = pltpu.get_barrier_semaphore()
    for k in range(1, n_t):
        pl.semaphore_signal(barrier, inc=1, device_id={"tensor": lax.rem(me + k, n_t)})
    n_z = n_s // 2
    z, core = slot // 2, lax.rem(slot, 2)
    sibling = 2 * z + 1 - core
    pl.semaphore_signal(barrier, inc=1, device_id={"dp": group + sibling})

    @pl.when(z > 0)
    def _():
        pl.semaphore_signal(barrier, inc=1, device_id={"dp": group + slot - 2})

    @pl.when(z < n_z - 1)
    def _():
        pl.semaphore_signal(barrier, inc=1, device_id={"dp": group + slot + 2})


    down_copy = local(1, down_in, dw)

    def voc_copy(c):
        part = pl.ds(pl.multiple_of(c * tile, tile), tile)
        return pltpu.make_async_copy(voc_in.at[part], voc.at[part], voc_sem.at[c])

    for c in range(n_v):
        voc_copy(c).start()
    gate_copy = local(2, gate_in, gu.at[:, pl.ds(0, f)])
    up_copy = local(3, up_in, gu.at[:, pl.ds(f, f)])
    tg[me] = jnp.broadcast_to(tgt[...], tg.shape[1:])
    beside = sum((z + n_z - q) // n_z + (2 * n_z - 1 - q - z) // n_z for q in (1,))
    pl.semaphore_wait(barrier, n_t + beside)

    def t_copy(kind, src, dst, to):
        return pltpu.make_async_remote_copy(
            src_ref=src, dst_ref=dst, send_sem=t_send.at[kind], recv_sem=t_recv.at[kind],
            device_id={"tensor": to},
        )

    def piece(kind, j, count=1):
        part = pl.ds(pl.multiple_of(j * rows, rows), count * rows)
        if kind == 0:
            return gram.at[pl.ds(1, n_t - 1), part, :]
        return w2.at[pl.ds(1, n_t - 1), part, pl.ds((kind - 1) * tile, tile)]

    def entered(stage):
        for sign, sem in ((-1, 0), (1, 1)):
            ahead = (n_z - 1 - z) if sign < 0 else z

            def tell():
                @pl.when(jnp.logical_and(ahead >= 1, ahead <= n_z - 2))
                def _():
                    pl.semaphore_signal(far_sem.at[sem], inc=1, device_id={"dp": group + slot + 2 * sign})

            if stage == 0:
                @pl.when(ahead == 1)
                def _():
                    tell()
            else:
                @pl.when(ahead >= 2)
                def _():
                    pl.semaphore_wait(far_sem.at[sem], 1)
                    tell()

    inner = jnp.logical_and(z > 0, z < n_z - 1)

    def s_remote(ref, family, kind, landing, to):
        return pltpu.make_async_remote_copy(
            src_ref=ref, dst_ref=ref, send_sem=s_send.at[family], recv_sem=s_recv.at[kind, landing],
            device_id={"dp": group + to},
        )

    def s_copy(kind, j, to):
        return s_remote(piece(kind, j), min(kind, 1), kind, n_z if to is sibling else j // 2, to)

    def s_ways(j, step, sign, act):
        if step == 0:
            for dist in range(3, n_z):
                for side in (-1, 1):
                    @pl.when(jnp.logical_and(z + side * dist >= 0, z + side * dist <= n_z - 1))
                    def _():
                        act(j, slot + 2 * side * dist)

            @pl.when(z > 0)
            def _():
                act(j, slot - 2)

            @pl.when(z < n_z - 1)
            def _():
                act(j, slot + 2)

            act(j, sibling)
        else:
            if step == 1:
                @pl.when(inner)
                def _():
                    act(j, slot - 2 * sign)

            act(j, sibling)

    def s_own(kind):
        s_ways(slot, 0, 0, lambda j, to: s_copy(kind, j, to).start())

    def s_relay(kind, step, relays):
        for sign in (-1, 1):
            there = jnp.logical_and(z + sign * step >= 0, z + sign * step <= n_z - 1)
            if step == 1:
                there = jnp.logical_and(there, inner if relays else jnp.logical_not(inner))

            @pl.when(there)
            def _():
                j = slot + 2 * sign * step
                s_remote(piece(kind, j), min(kind, 1), kind, j // 2, sibling).wait_recv()
                s_ways(j, step, sign, lambda j, to: s_copy(kind, j, to).start())

    def s_arrived(kind):
        every = piece(kind, 0, n_z)
        s_remote(every, 0, kind, n_z, sibling).wait_recv()

    def s_sent(family):
        for place in range(n_z):
            others = [abs(place - q) for q in range(n_z) if q != place]
            count = sum(q == 1 or q >= 3 for q in others) + n_z + (2 if 0 < place < n_z - 1 else 0)

            @pl.when(z == place)
            def _():
                every = (w2 if family else gram).at[pl.ds(1, n_t - 1), pl.ds(0, count * rows), :]
                s_remote(every, family, family, n_z, sibling).wait_send()

    def block(k):
        return lax.rem(me + k, n_t)

    def t_start(kind, src, dst, buf):
        targets = (far, x_near, y_near) if relayed else [block(k) for k in range(1, n_t)]
        for to in targets:
            t_copy(kind, src(to), dst(to), to).start()
        others = buf.at[pl.ds(1, n_t - 1)]
        return t_copy(kind, others, others, block(1))

    relayed = n_t == 4
    if relayed:
        y, x = me // 2, lax.rem(me, 2)
        x_near, y_near, far = 2 * y + 1 - x, 2 * (1 - y) + x, 2 * (1 - y) + 1 - x

    def half(ref, h):
        return ref.at[:, pl.ds(h * (d // 2), d // 2)]

    def r_copies(kind, src, buf, place):
        plan = (
            (half(src, 0), me, 0, x_near), (half(src, 1), me, 1, x_near),
            (half(src, 1), me, 1, y_near), (half(src, 0), me, 0, y_near),
            (half(buf.at[place(y_near, me)], 1), y_near, 1, x_near),
            (half(buf.at[place(x_near, me)], 0), x_near, 0, y_near),
        )
        def remote(src, dst, group_index, to):
            return pltpu.make_async_remote_copy(
                src_ref=src, dst_ref=dst, send_sem=r_send.at[kind], recv_sem=r_recv.at[kind, group_index],
                device_id={"tensor": to},
            )

        copies = [
            remote(part, half(buf.at[place(owner, to)], h), (0, 2, 1, 2, 3, 3)[i], to)
            for i, (part, owner, h, to) in enumerate(plan)
        ]
        one, three = buf.at[0], buf.at[pl.ds(0, 3)]
        return copies, [remote(one, one, i, x_near) for i in (2, 3)], remote(three, three, 0, x_near)

    def r_start(copies):
        for i in (0, 2, 1, 3):
            copies[0][i].start()

    def r_pass(copies):
        copies[0][0].wait_recv()
        copies[0][5].start()
        copies[0][2].wait_recv()
        copies[0][4].start()

    down_rows = down_in.at[own_rows]
    if relayed:
        sl_copies = r_copies(0, down_rows, sl, lambda owner, to: lax.rem(owner - to + n_t, n_t))
        tok_copies = r_copies(1, tok_in, tok, lambda owner, to: owner)
        r_start(sl_copies)
    else:
        sl_copies = t_start(4, lambda to: down_rows, lambda to: sl.at[lax.rem(me - to + n_t, n_t)], sl)
        tok_copies = t_start(5, lambda k: tok_in, lambda k: tok.at[me], tok)

    def token_block(index):
        part = pl.ds(pl.multiple_of(index * tl, tl), tl)
        x = tok[index].astype(F32)
        square = jnp.sum(x * x, axis=1, keepdims=True)
        x2[part, :] = jnp.broadcast_to(square, (tl, x2.shape[1]))
        xn[part, :] = (x * lax.rsqrt(square * (1.0 / d) + EPS) * ng[...]).astype(BF16)
        xg[part, :] = (x * (fg[...] * SHRINK)).astype(BF16)

    if n_z > 3:
        entered(0)
    own_tok.wait()
    token_block(me)
    down_copy.wait()
    sgo[...] = (dw[...].astype(F32) * (fg[...] * SHRINK)).astype(BF16)

    def own_w2(c):
        voc_copy(c).wait()
        part = pl.ds(c * tile, tile)
        w2[0, :, part] = dot_nt(sgo[...], voc[part, :]).astype(BF16)

    own_w2(0)
    if relayed:
        r_pass(sl_copies)
        r_start(tok_copies)
    own_w2(1)
    if n_z > 3:
        entered(1)
    for c in range(2, n_v):
        own_w2(c)
    tg_copies = t_start(0, lambda k: tg.at[me], lambda k: tg.at[me], tg)
    own_gram = dot_nt(dw[...], dw[...])
    own_high = own_gram.astype(BF16)
    gram[0] = own_high
    glow[...] = (own_gram - own_high.astype(F32)).astype(BF16)

    if relayed:
        for copy in sl_copies[1]:
            copy.wait_recv()
    else:
        sl_copies.wait_recv()
    raw = sl[pl.ds(1, n_t - 1)].reshape((n_t - 1) * rows, d)
    gram[pl.ds(1, n_t - 1), own_rows, :] = dot_nt(raw, dw[...]).astype(BF16).reshape(n_t - 1, rows, f)
    s_own(0)
    sg[...] = (raw.astype(F32) * (fg[...] * SHRINK)).astype(BF16)
    for c in range(n_v):
        part = pl.ds(c * tile, tile)
        w2[pl.ds(1, n_t - 1), own_rows, part] = dot_nt(sg[...], voc[part, :]).astype(BF16).reshape(n_t - 1, rows, tile)
        s_own(1 + c)
        if relayed and c == 0:
            r_pass(tok_copies)

    kinds = range(n_v + 1)

    def gate_up():
        gate_copy.wait()
        up_copy.wait()
        both = dot(xn[...], gu[...])
        gate, up = both[:, :f], both[:, f:]
        hid[me] = (gate / (1.0 + jnp.exp(-gate)) * up).astype(BF16)
        return t_start(1, lambda k: hid.at[me], lambda k: hid.at[me], hid)

    def token_logits(c):
        part = pl.ds(c * tile, tile)
        logit[:, part] = dot_nt(xg[...], voc[part, :])

    steps = range(1, n_z)
    pairs = [(kind, step) for kind in kinds for step in steps]
    inner_order = [(kind, 1) for kind in kinds]
    end_order = sorted(pairs, key=lambda e: (e[0] > 0, e[0] + 2 * e[1]))

    def relay(count, end_count):
        for order, n, relays in ((inner_order, count, True), (end_order, end_count, False)):
            for kind, step in order[:n]:
                s_relay(kind, step, relays)
            del order[:n]

    if relayed:
        tok_copies[1][0].wait_recv()
        token_block(x_near)
        token_block(y_near)
        relay(3, 0)
        tok_copies[1][1].wait_recv()
        token_block(far)
    else:
        tok_copies.wait_recv()
        for k in range(1, n_t):
            token_block(lax.rem(me + n_t - k, n_t))
        relay(3, 0)
    h_copies = gate_up()
    relay(1, 0)
    cross[...] = dot_nt(tok[...].reshape(total, d), dw[...])
    relay(0, 0)
    token_logits(0)
    relay(0, 0)
    for c in range(1, n_v - 1):
        token_logits(c)
    relay(0, 3)
    tg_copies.wait_recv()
    for t in range(n_t):
        tgc[pl.ds(t * tl, tl), :] = jnp.broadcast_to(to_column(tg[t][0:1, :]), (tl, tgc.shape[1]))
    h_copies.wait_recv()
    for kind, step in pairs:
        if kind == 0 and (kind, step) in inner_order:
            s_relay(kind, step, True)
            inner_order.remove((kind, step))
        if kind == 0 and (kind, step) in end_order:
            s_relay(kind, step, False)
            end_order.remove((kind, step))
    s_arrived(0)
    hidden = jnp.concatenate([hid[block(k)] for k in range(n_t)], axis=1)
    pulled = dot(hidden, gram[...].reshape(n_t * f, f)) + dot(hid[me], glow[...])
    share = jnp.sum(hid[me].astype(F32) * (2.0 * cross[...] + pulled), axis=1, keepdims=True)
    qs[me] = jnp.broadcast_to(to_row(share), qs.shape[1:])
    q_copies = t_start(2, lambda k: qs.at[me], lambda k: qs.at[me], qs)

    relay(len(inner_order), 0)
    token_logits(n_v - 1)
    relay(0, len(end_order))
    for c in range(n_v):
        s_arrived(1 + c)
        part = pl.ds(c * tile, tile)
        logit[:, part] += dot(hidden, w2[:, :, part].reshape(n_t * f, tile))

    @pl.loop(0, n_t, unroll=min(n_t, 4))
    def _(t):
        part = pl.ds(pl.multiple_of(t * tl, tl), tl)
        raw_logit = logit[part, :]
        top = jnp.max(raw_logit, axis=1, keepdims=True)
        columns = lax.broadcasted_iota(jnp.int32, (tl, v), 1) + me * v
        hit = jnp.sum(jnp.where(columns == tgc[part, 0:1], raw_logit, 0.0), axis=1, keepdims=True)
        logit[part, :] = raw_logit - top
        sts[t, 0:1, :] = to_row(top)
        sts[t, 2:3, :] = to_row(hit)

    q_copies.wait_recv()
    pulls = qs[0, 0:1, :]
    for t in range(1, n_t):
        pulls = pulls + qs[t, 0:1, :]

    square = jnp.maximum(x2[:, 0:1] + to_column(pulls), 0.0)
    scale = lax.rsqrt(square * (1.0 / d) + EPS) * GROW
    x2[...] = jnp.broadcast_to(scale, x2.shape)

    @pl.loop(0, n_t, unroll=min(n_t, 4))
    def _(t):
        part = pl.ds(pl.multiple_of(t * tl, tl), tl)
        grow = x2[part, 0:1]
        mass = jnp.sum(jnp.exp(logit[part, :] * grow), axis=1, keepdims=True)
        row = to_row(grow)
        sts[t, 0:1, :] = sts[t, 0:1, :] * row
        sts[t, 1:2, :] = to_row(mass)
        sts[t, 2:3, :] = sts[t, 2:3, :] * row

    end = t_start(3, lambda to: sts.at[to], lambda to: sta.at[me], sta)
    sta[me] = sts[me]
    positions = me * tl + lax.broadcasted_iota(jnp.int32, (1, tl), 1)
    packs = positions // PACK_LEN
    limits = jnp.zeros((1, tl), jnp.int32)
    for i in range(lens.shape[0]):
        limits = jnp.where(packs == i, lens[i], limits)
    end.wait_recv()
    stats = [sta[t] for t in range(n_t)]
    top = stats[0][0:1, :]
    for s in stats[1:]:
        top = jnp.maximum(top, s[0:1, :])
    mass = sum(s[1:2, :] * jnp.exp(s[0:1, :] - top) for s in stats)
    hit = sum(s[2:3, :] for s in stats)
    out[...] = jnp.where(positions - packs * PACK_LEN < limits, top + jnp.log(mass) - hit, 0.0)

    for copy in (sl_copies, tok_copies):
        (copy[2] if relayed else copy).wait_send()
    for copy in (tg_copies, h_copies, q_copies, end):
        copy.wait_send()
    for family in (0, 1):
        s_sent(family)


def body(n_t, n_dp, tokens, norm_gain, gate_w, up_w, down_w, final_gain, vocab_w, targets, lengths):
    tl, d = tokens.shape
    f = down_w.shape[0]
    v = vocab_w.shape[0]
    n_s = min(n_dp, f // 16)
    n_z = n_s // 2
    rows = f // n_s
    total = n_t * tl
    tile = next(size for size in (384, 256, 128) if v % size == 0)
    vmem = pl.BlockSpec(memory_space=pltpu.VMEM)
    hbm = pl.BlockSpec(memory_space=pl.ANY)
    losses = pl.pallas_call(
        functools.partial(kernel, n_t, n_s, tile),
        out_shape=jax.ShapeDtypeStruct((1, tl), F32),
        in_specs=[hbm, vmem, hbm, hbm, hbm, vmem, hbm, vmem, pl.BlockSpec(memory_space=pltpu.SMEM)],
        out_specs=vmem,
        scratch_shapes=[
            pltpu.VMEM((n_t, tl, d), BF16),
            pltpu.VMEM((n_t, rows, d), BF16),
            pltpu.VMEM((d, 2 * f), BF16),
            pltpu.VMEM((f, d), BF16),
            pltpu.VMEM((v, d), BF16),
            pltpu.VMEM((total, d), BF16),
            pltpu.VMEM((total, d), BF16),
            pltpu.VMEM(((n_t - 1) * rows, d), BF16),
            pltpu.VMEM((f, d), BF16),
            pltpu.VMEM((total, 128), F32),
            pltpu.VMEM((total, f), F32),
            pltpu.VMEM((total, v), F32),
            pltpu.VMEM((n_t, f, v), BF16),
            pltpu.VMEM((n_t, f, f), BF16),
            pltpu.VMEM((f, f), BF16),
            pltpu.VMEM((n_t, 8, tl), jnp.int32),
            pltpu.VMEM((total, 128), jnp.int32),
            pltpu.VMEM((n_t, total, f), BF16),
            pltpu.VMEM((n_t, 8, total), F32),
            pltpu.VMEM((n_t, 8, tl), F32),
            pltpu.VMEM((n_t, 8, tl), F32),
            pltpu.SemaphoreType.DMA((4,)),
            pltpu.SemaphoreType.DMA((v // tile,)),
            pltpu.SemaphoreType.DMA((4 if n_t == 4 else 6,)),
            pltpu.SemaphoreType.DMA((4 if n_t == 4 else 6,)),
            pltpu.SemaphoreType.DMA((2,)),
            pltpu.SemaphoreType.DMA((2, 4)),
            pltpu.SemaphoreType.DMA((2,)),
            pltpu.SemaphoreType.DMA((1 + v // tile, n_z + 1)),
            pltpu.SemaphoreType.REGULAR((2,)),
        ],
        compiler_params=pltpu.CompilerParams(
            collective_id=0, has_side_effects=True, vmem_limit_bytes=60 * 1024 * 1024
        ),
    )(
        tokens, norm_gain.reshape(1, d), gate_w, up_w, down_w, final_gain.reshape(1, d), vocab_w,
        targets.reshape(1, tl), lengths,
    )
    return losses.reshape(tl)


def solution(mesh):
    return jax.shard_map(
        functools.partial(body, mesh.shape["tensor"], mesh.shape["dp"]),
        mesh=mesh,
        in_specs=(
            P(("dp", "tensor"), None),
            P(),
            P(None, "tensor"),
            P(None, "tensor"),
            P("tensor", None),
            P(),
            P("tensor", None),
            P(("dp", "tensor")),
            P("dp"),
        ),
        out_specs=P(("dp", "tensor")),
        check_vma=False,
    )
```

```python
import functools

import jax
import jax.numpy as jnp
from jax import lax
from jax.experimental import pallas as pl
from jax.experimental.pallas import tpu as pltpu
from jax.sharding import PartitionSpec as P

PACK_LEN = 128
EPS = 1e-06
SHRINK = 2.0**-27
GROW = 2.0**27
F32, BF16 = jnp.float32, jnp.bfloat16
NT = (((1,), (1,)), ((), ()))


def dot(a, b):
    return jnp.dot(a, b, preferred_element_type=F32)


def dot_nt(a, b):
    return lax.dot_general(a, b, NT, preferred_element_type=F32)


def diagonal(rows):
    shape = (rows, rows)
    return lax.broadcasted_iota(jnp.int32, shape, 0) == lax.broadcasted_iota(jnp.int32, shape, 1)


def to_column(row):
    n = row.shape[1]
    return jnp.sum(jnp.where(diagonal(n), row, jnp.zeros_like(row)), axis=1, keepdims=True)


def to_row(column):
    n = column.shape[0]
    return jnp.sum(jnp.where(diagonal(n), column, jnp.zeros_like(column)), axis=0, keepdims=True)


def kernel(
    n_t, n_s, tile,
    tok_in, ng, gate_in, up_in, down_in, fg, voc_in, tgt, lens,
    out,
    tok, sl, gu, dw, voc, xn, xg, sg, sgo, x2, cross, logit, w2, gram, glow, tg, tgc, hid, qs, sts, sta,
    local_sem, voc_sem, t_send, t_recv, r_send, r_recv, s_send, s_recv, far_sem,
):
    me = lax.axis_index("tensor")
    dp = lax.axis_index("dp")
    slot = lax.rem(dp, n_s)
    group = dp - slot
    _, tl, d = tok.shape
    rows = sl.shape[1]
    f = dw.shape[0]
    v = voc.shape[0]
    total = n_t * tl
    n_v = v // tile

    def local(i, src, dst):
        copy = pltpu.make_async_copy(src, dst, local_sem.at[i])
        copy.start()
        return copy

    own_rows = pl.ds(pl.multiple_of(slot * rows, rows), rows)
    own_tok = local(0, tok_in, tok.at[me])

    barrier = pltpu.get_barrier_semaphore()
    for k in range(1, n_t):
        pl.semaphore_signal(barrier, inc=1, device_id={"tensor": lax.rem(me + k, n_t)})
    n_z = n_s // 2
    z, core = slot // 2, lax.rem(slot, 2)
    sibling = 2 * z + 1 - core
    pl.semaphore_signal(barrier, inc=1, device_id={"dp": group + sibling})

    @pl.when(z > 0)
    def _():
        pl.semaphore_signal(barrier, inc=1, device_id={"dp": group + slot - 2})

    @pl.when(z < n_z - 1)
    def _():
        pl.semaphore_signal(barrier, inc=1, device_id={"dp": group + slot + 2})


    down_copy = local(1, down_in, dw)

    def voc_copy(c):
        part = pl.ds(pl.multiple_of(c * tile, tile), tile)
        return pltpu.make_async_copy(voc_in.at[part], voc.at[part], voc_sem.at[c])

    for c in range(n_v):
        voc_copy(c).start()
    gate_copy = local(2, gate_in, gu.at[:, pl.ds(0, f)])
    up_copy = local(3, up_in, gu.at[:, pl.ds(f, f)])
    tg[me] = jnp.broadcast_to(tgt[...], tg.shape[1:])
    beside = sum((z + n_z - q) // n_z + (2 * n_z - 1 - q - z) // n_z for q in (1,))
    pl.semaphore_wait(barrier, n_t + beside)

    def t_copy(kind, src, dst, to):
        return pltpu.make_async_remote_copy(
            src_ref=src, dst_ref=dst, send_sem=t_send.at[kind], recv_sem=t_recv.at[kind],
            device_id={"tensor": to},
        )

    def piece(kind, j, count=1):
        part = pl.ds(pl.multiple_of(j * rows, rows), count * rows)
        if kind == 0:
            return gram.at[pl.ds(1, n_t - 1), part, :]
        return w2.at[pl.ds(1, n_t - 1), part, pl.ds((kind - 1) * tile, tile)]

    def entered(stage):
        for sign, sem in ((-1, 0), (1, 1)):
            ahead = (n_z - 1 - z) if sign < 0 else z

            def tell():
                @pl.when(jnp.logical_and(ahead >= 1, ahead <= n_z - 2))
                def _():
                    pl.semaphore_signal(far_sem.at[sem], inc=1, device_id={"dp": group + slot + 2 * sign})

            if stage == 0:
                @pl.when(ahead == 1)
                def _():
                    tell()
            else:
                @pl.when(ahead >= 2)
                def _():
                    pl.semaphore_wait(far_sem.at[sem], 1)
                    tell()

    inner = jnp.logical_and(z > 0, z < n_z - 1)

    def s_remote(ref, family, kind, landing, to):
        return pltpu.make_async_remote_copy(
            src_ref=ref, dst_ref=ref, send_sem=s_send.at[family], recv_sem=s_recv.at[kind, landing],
            device_id={"dp": group + to},
        )

    def s_copy(kind, j, to):
        return s_remote(piece(kind, j), min(kind, 1), kind, n_z if to is sibling else j // 2, to)

    def s_ways(j, step, sign, act):
        if step == 0:
            for dist in range(3, n_z):
                for side in (-1, 1):
                    @pl.when(jnp.logical_and(z + side * dist >= 0, z + side * dist <= n_z - 1))
                    def _():
                        act(j, slot + 2 * side * dist)

            @pl.when(z > 0)
            def _():
                act(j, slot - 2)

            @pl.when(z < n_z - 1)
            def _():
                act(j, slot + 2)

            act(j, sibling)
        else:
            if step == 1:
                @pl.when(inner)
                def _():
                    act(j, slot - 2 * sign)

            act(j, sibling)

    def s_own(kind):
        s_ways(slot, 0, 0, lambda j, to: s_copy(kind, j, to).start())

    def s_relay(kind, step, relays):
        for sign in (-1, 1):
            there = jnp.logical_and(z + sign * step >= 0, z + sign * step <= n_z - 1)
            if step == 1:
                there = jnp.logical_and(there, inner if relays else jnp.logical_not(inner))

            @pl.when(there)
            def _():
                j = slot + 2 * sign * step
                s_remote(piece(kind, j), min(kind, 1), kind, j // 2, sibling).wait_recv()
                s_ways(j, step, sign, lambda j, to: s_copy(kind, j, to).start())

    def s_arrived(kind):
        every = piece(kind, 0, n_z)
        s_remote(every, 0, kind, n_z, sibling).wait_recv()

    def s_sent(family):
        for place in range(n_z):
            others = [abs(place - q) for q in range(n_z) if q != place]
            count = sum(q == 1 or q >= 3 for q in others) + n_z + (2 if 0 < place < n_z - 1 else 0)

            @pl.when(z == place)
            def _():
                every = (w2 if family else gram).at[pl.ds(1, n_t - 1), pl.ds(0, count * rows), :]
                s_remote(every, family, family, n_z, sibling).wait_send()

    def block(k):
        return lax.rem(me + k, n_t)

    def t_start(kind, src, dst, buf):
        targets = (far, x_near, y_near) if relayed else [block(k) for k in range(1, n_t)]
        for to in targets:
            t_copy(kind, src(to), dst(to), to).start()
        others = buf.at[pl.ds(1, n_t - 1)]
        return t_copy(kind, others, others, block(1))

    relayed = n_t == 4
    if relayed:
        y, x = me // 2, lax.rem(me, 2)
        x_near, y_near, far = 2 * y + 1 - x, 2 * (1 - y) + x, 2 * (1 - y) + 1 - x

    def half(ref, h):
        return ref.at[:, pl.ds(h * (d // 2), d // 2)]

    def r_copies(kind, src, buf, place):
        plan = (
            (half(src, 0), me, 0, x_near), (half(src, 1), me, 1, x_near),
            (half(src, 1), me, 1, y_near), (half(src, 0), me, 0, y_near),
            (half(buf.at[place(y_near, me)], 1), y_near, 1, x_near),
            (half(buf.at[place(x_near, me)], 0), x_near, 0, y_near),
        )
        def remote(src, dst, group_index, to):
            return pltpu.make_async_remote_copy(
                src_ref=src, dst_ref=dst, send_sem=r_send.at[kind], recv_sem=r_recv.at[kind, group_index],
                device_id={"tensor": to},
            )

        copies = [
            remote(part, half(buf.at[place(owner, to)], h), (0, 2, 1, 2, 3, 3)[i], to)
            for i, (part, owner, h, to) in enumerate(plan)
        ]
        one, three = buf.at[0], buf.at[pl.ds(0, 3)]
        return copies, [remote(one, one, i, x_near) for i in (2, 3)], remote(three, three, 0, x_near)

    def r_start(copies):
        for i in (0, 2, 1, 3):
            copies[0][i].start()

    def r_pass(copies):
        copies[0][0].wait_recv()
        copies[0][5].start()
        copies[0][2].wait_recv()
        copies[0][4].start()

    down_rows = down_in.at[own_rows]
    if relayed:
        sl_copies = r_copies(0, down_rows, sl, lambda owner, to: lax.rem(owner - to + n_t, n_t))
        tok_copies = r_copies(1, tok_in, tok, lambda owner, to: owner)
        r_start(sl_copies)
    else:
        sl_copies = t_start(4, lambda to: down_rows, lambda to: sl.at[lax.rem(me - to + n_t, n_t)], sl)
        tok_copies = t_start(5, lambda k: tok_in, lambda k: tok.at[me], tok)

    def token_block(index):
        part = pl.ds(pl.multiple_of(index * tl, tl), tl)
        x = tok[index].astype(F32)
        square = jnp.sum(x * x, axis=1, keepdims=True)
        x2[part, :] = jnp.broadcast_to(square, (tl, x2.shape[1]))
        xn[part, :] = (x * lax.rsqrt(square * (1.0 / d) + EPS) * ng[...]).astype(BF16)
        xg[part, :] = (x * (fg[...] * SHRINK)).astype(BF16)

    if n_z > 3:
        entered(0)
    own_tok.wait()
    token_block(me)
    down_copy.wait()
    sgo[...] = (dw[...].astype(F32) * (fg[...] * SHRINK)).astype(BF16)

    def own_w2(c):
        voc_copy(c).wait()
        part = pl.ds(c * tile, tile)
        w2[0, :, part] = dot_nt(sgo[...], voc[part, :]).astype(BF16)

    own_w2(0)
    if relayed:
        r_pass(sl_copies)

        @pl.when(core == 1)
        def _():
            r_start(tok_copies)

    own_w2(1)
    if relayed:
        @pl.when(core == 0)
        def _():
            r_start(tok_copies)

    if n_z > 3:
        entered(1)
    for c in range(2, n_v):
        own_w2(c)
    tg_copies = t_start(0, lambda k: tg.at[me], lambda k: tg.at[me], tg)
    own_gram = dot_nt(dw[...], dw[...])
    own_high = own_gram.astype(BF16)
    gram[0] = own_high
    glow[...] = (own_gram - own_high.astype(F32)).astype(BF16)

    if relayed:
        for copy in sl_copies[1]:
            copy.wait_recv()
    else:
        sl_copies.wait_recv()
    raw = sl[pl.ds(1, n_t - 1)].reshape((n_t - 1) * rows, d)
    gram[pl.ds(1, n_t - 1), own_rows, :] = dot_nt(raw, dw[...]).astype(BF16).reshape(n_t - 1, rows, f)
    s_own(0)
    sg[...] = (raw.astype(F32) * (fg[...] * SHRINK)).astype(BF16)
    for c in range(n_v):
        part = pl.ds(c * tile, tile)
        w2[pl.ds(1, n_t - 1), own_rows, part] = dot_nt(sg[...], voc[part, :]).astype(BF16).reshape(n_t - 1, rows, tile)
        s_own(1 + c)
        if relayed and c == 0:
            r_pass(tok_copies)

    kinds = range(n_v + 1)

    def gate_up():
        gate_copy.wait()
        up_copy.wait()
        both = dot(xn[...], gu[...])
        gate, up = both[:, :f], both[:, f:]
        hid[me] = (gate / (1.0 + jnp.exp(-gate)) * up).astype(BF16)
        return t_start(1, lambda k: hid.at[me], lambda k: hid.at[me], hid)

    def token_logits(c):
        part = pl.ds(c * tile, tile)
        logit[:, part] = dot_nt(xg[...], voc[part, :])

    steps = range(1, n_z)
    pairs = [(kind, step) for kind in kinds for step in steps]
    inner_order = [(kind, 1) for kind in kinds]
    end_order = sorted(pairs, key=lambda e: (e[0] > 0, e[0] + 2 * e[1]))

    def relay(count, end_count):
        for order, n, relays in ((inner_order, count, True), (end_order, end_count, False)):
            for kind, step in order[:n]:
                s_relay(kind, step, relays)
            del order[:n]

    if relayed:
        tok_copies[1][0].wait_recv()
        token_block(x_near)
        token_block(y_near)
        relay(3, 0)
        tok_copies[1][1].wait_recv()
        token_block(far)
    else:
        tok_copies.wait_recv()
        for k in range(1, n_t):
            token_block(lax.rem(me + n_t - k, n_t))
        relay(3, 0)
    h_copies = gate_up()
    relay(1, 0)
    cross[...] = dot_nt(tok[...].reshape(total, d), dw[...])
    relay(0, 0)
    token_logits(0)
    relay(0, 0)
    for c in range(1, n_v - 1):
        token_logits(c)
    relay(0, 3)
    tg_copies.wait_recv()
    for t in range(n_t):
        tgc[pl.ds(t * tl, tl), :] = jnp.broadcast_to(to_column(tg[t][0:1, :]), (tl, tgc.shape[1]))
    h_copies.wait_recv()
    for kind, step in pairs:
        if kind == 0 and (kind, step) in inner_order:
            s_relay(kind, step, True)
            inner_order.remove((kind, step))
        if kind == 0 and (kind, step) in end_order:
            s_relay(kind, step, False)
            end_order.remove((kind, step))
    s_arrived(0)
    hidden = jnp.concatenate([hid[block(k)] for k in range(n_t)], axis=1)
    pulled = dot(hidden, gram[...].reshape(n_t * f, f)) + dot(hid[me], glow[...])
    share = jnp.sum(hid[me].astype(F32) * (2.0 * cross[...] + pulled), axis=1, keepdims=True)
    qs[me] = jnp.broadcast_to(to_row(share), qs.shape[1:])
    q_copies = t_start(2, lambda k: qs.at[me], lambda k: qs.at[me], qs)

    relay(len(inner_order), 0)
    token_logits(n_v - 1)
    relay(0, len(end_order))
    for c in range(n_v):
        s_arrived(1 + c)
        part = pl.ds(c * tile, tile)
        logit[:, part] += dot(hidden, w2[:, :, part].reshape(n_t * f, tile))

    @pl.loop(0, n_t, unroll=min(n_t, 4))
    def _(t):
        part = pl.ds(pl.multiple_of(t * tl, tl), tl)
        raw_logit = logit[part, :]
        top = jnp.max(raw_logit, axis=1, keepdims=True)
        columns = lax.broadcasted_iota(jnp.int32, (tl, v), 1) + me * v
        hit = jnp.sum(jnp.where(columns == tgc[part, 0:1], raw_logit, 0.0), axis=1, keepdims=True)
        logit[part, :] = raw_logit - top
        sts[t, 0:1, :] = to_row(top)
        sts[t, 2:3, :] = to_row(hit)

    q_copies.wait_recv()
    pulls = qs[0, 0:1, :]
    for t in range(1, n_t):
        pulls = pulls + qs[t, 0:1, :]

    square = jnp.maximum(x2[:, 0:1] + to_column(pulls), 0.0)
    scale = lax.rsqrt(square * (1.0 / d) + EPS) * GROW
    x2[...] = jnp.broadcast_to(scale, x2.shape)

    @pl.loop(0, n_t, unroll=min(n_t, 4))
    def _(t):
        part = pl.ds(pl.multiple_of(t * tl, tl), tl)
        grow = x2[part, 0:1]
        mass = jnp.sum(jnp.exp(logit[part, :] * grow), axis=1, keepdims=True)
        row = to_row(grow)
        sts[t, 0:1, :] = sts[t, 0:1, :] * row
        sts[t, 1:2, :] = to_row(mass)
        sts[t, 2:3, :] = sts[t, 2:3, :] * row

    end = t_start(3, lambda to: sts.at[to], lambda to: sta.at[me], sta)
    sta[me] = sts[me]
    positions = me * tl + lax.broadcasted_iota(jnp.int32, (1, tl), 1)
    packs = positions // PACK_LEN
    limits = jnp.zeros((1, tl), jnp.int32)
    for i in range(lens.shape[0]):
        limits = jnp.where(packs == i, lens[i], limits)
    end.wait_recv()
    stats = [sta[t] for t in range(n_t)]
    top = stats[0][0:1, :]
    for s in stats[1:]:
        top = jnp.maximum(top, s[0:1, :])
    mass = sum(s[1:2, :] * jnp.exp(s[0:1, :] - top) for s in stats)
    hit = sum(s[2:3, :] for s in stats)
    out[...] = jnp.where(positions - packs * PACK_LEN < limits, top + jnp.log(mass) - hit, 0.0)

    for copy in (sl_copies, tok_copies):
        (copy[2] if relayed else copy).wait_send()
    for copy in (tg_copies, h_copies, q_copies, end):
        copy.wait_send()
    for family in (0, 1):
        s_sent(family)


def body(n_t, n_dp, tokens, norm_gain, gate_w, up_w, down_w, final_gain, vocab_w, targets, lengths):
    tl, d = tokens.shape
    f = down_w.shape[0]
    v = vocab_w.shape[0]
    n_s = min(n_dp, f // 16)
    n_z = n_s // 2
    rows = f // n_s
    total = n_t * tl
    tile = next(size for size in (384, 256, 128) if v % size == 0)
    vmem = pl.BlockSpec(memory_space=pltpu.VMEM)
    hbm = pl.BlockSpec(memory_space=pl.ANY)
    losses = pl.pallas_call(
        functools.partial(kernel, n_t, n_s, tile),
        out_shape=jax.ShapeDtypeStruct((1, tl), F32),
        in_specs=[hbm, vmem, hbm, hbm, hbm, vmem, hbm, vmem, pl.BlockSpec(memory_space=pltpu.SMEM)],
        out_specs=vmem,
        scratch_shapes=[
            pltpu.VMEM((n_t, tl, d), BF16),
            pltpu.VMEM((n_t, rows, d), BF16),
            pltpu.VMEM((d, 2 * f), BF16),
            pltpu.VMEM((f, d), BF16),
            pltpu.VMEM((v, d), BF16),
            pltpu.VMEM((total, d), BF16),
            pltpu.VMEM((total, d), BF16),
            pltpu.VMEM(((n_t - 1) * rows, d), BF16),
            pltpu.VMEM((f, d), BF16),
            pltpu.VMEM((total, 128), F32),
            pltpu.VMEM((total, f), F32),
            pltpu.VMEM((total, v), F32),
            pltpu.VMEM((n_t, f, v), BF16),
            pltpu.VMEM((n_t, f, f), BF16),
            pltpu.VMEM((f, f), BF16),
            pltpu.VMEM((n_t, 8, tl), jnp.int32),
            pltpu.VMEM((total, 128), jnp.int32),
            pltpu.VMEM((n_t, total, f), BF16),
            pltpu.VMEM((n_t, 8, total), F32),
            pltpu.VMEM((n_t, 8, tl), F32),
            pltpu.VMEM((n_t, 8, tl), F32),
            pltpu.SemaphoreType.DMA((4,)),
            pltpu.SemaphoreType.DMA((v // tile,)),
            pltpu.SemaphoreType.DMA((4 if n_t == 4 else 6,)),
            pltpu.SemaphoreType.DMA((4 if n_t == 4 else 6,)),
            pltpu.SemaphoreType.DMA((2,)),
            pltpu.SemaphoreType.DMA((2, 4)),
            pltpu.SemaphoreType.DMA((2,)),
            pltpu.SemaphoreType.DMA((1 + v // tile, n_z + 1)),
            pltpu.SemaphoreType.REGULAR((2,)),
        ],
        compiler_params=pltpu.CompilerParams(
            collective_id=0, has_side_effects=True, vmem_limit_bytes=60 * 1024 * 1024
        ),
    )(
        tokens, norm_gain.reshape(1, d), gate_w, up_w, down_w, final_gain.reshape(1, d), vocab_w,
        targets.reshape(1, tl), lengths,
    )
    return losses.reshape(tl)


def solution(mesh):
    return jax.shard_map(
        functools.partial(body, mesh.shape["tensor"], mesh.shape["dp"]),
        mesh=mesh,
        in_specs=(
            P(("dp", "tensor"), None),
            P(),
            P(None, "tensor"),
            P(None, "tensor"),
            P("tensor", None),
            P(),
            P("tensor", None),
            P(("dp", "tensor")),
            P("dp"),
        ),
        out_specs=P(("dp", "tensor")),
        check_vma=False,
    )
```
